32 devices in a mesh: gx: 4 (over z), gy: 2 (over y), gz: 4 (over x, core).
Axes of the slice: x: 2, y: 2, z: 4, core: 2. Of those that a mesh axis runs over, the one named last changes fastest.
Arguments:
- features: bfloat16 [32, 16, 8, 512], P(None, 'gx', 'gy', 'gz'), may hold values from -6 to 6
- cotangent: bfloat16 [32, 16, 8, 512], P(None, 'gx', 'gy', 'gz'), may hold values from -6 to 6
- w_fine_in: bfloat16 [27, 32, 32], replicated, may hold values from -0.21875 to 0.21875
- w_coarse_in: bfloat16 [27, 32, 128], replicated, may hold values from -0.21875 to 0.21875
- w_coarse_mid: bfloat16 [27, 128, 128], replicated, may hold values from -0.109375 to 0.109375
- w_lift: bfloat16 [128, 32], replicated, may hold values from -0.5 to 0.5
- w_fine_out: bfloat16 [27, 32, 32], replicated, may hold values from -0.21875 to 0.21875
Outputs:
- output: bfloat16 [32, 16, 8, 512], P(None, 'gx', 'gy', 'gz')
- grad_input: bfloat16 [32, 16, 8, 512], P(None, 'gx', 'gy', 'gz')
- grad_fine_in: float32 [27, 32, 32], P(None, 'gx', ('gy', 'gz'))
- grad_coarse_in: float32 [27, 32, 128], P(None, 'gx', ('gy', 'gz'))
- grad_coarse_mid: float32 [27, 128, 128], P(None, 'gx', ('gy', 'gz'))
- grad_lift: float32 [128, 32], P('gx', ('gy', 'gz'))
- grad_fine_out: float32 [27, 32, 32], P(None, 'gx', ('gy', 'gz'))
The draws below stay inside these ranges and needn't reach their ends.
All inputs are finite; a program needn't handle non-finite values.
Results may differ from the reference program's by a relative error of at most 0.02.
Values may be sent and summed in bfloat16 or wider, within the bound.
A program may use at most 128 MiB of HBM per device.

```python
import math
import jax
import jax.numpy as jnp
from jax import lax

C = 32
CC = 128
NX = 16
NY = 8
NZ = 512


def levels(rng, dims, shards, least, top_value):
    loudness = 1.0
    for axis_at, shards_of in shards:
        heights = jax.random.uniform(jax.random.fold_in(jax.random.fold_in(rng, 6), axis_at), (shards_of,), jnp.float32, least / len(shards), top_value / len(shards))
        loudness = loudness * jnp.repeat(jnp.exp(heights), dims[axis_at] // shards_of).reshape((-1,) + (1,) * (len(dims) - 1 - axis_at))
    return loudness


def scatter_about(rng, shape, scale, reach, pieces=(), kind=jnp.bfloat16):
    values = jax.random.normal(rng, shape, jnp.float32) * scale
    if len(pieces) > 0:
        values = levels(rng, shape, pieces, -0.22, 0.18) * values
    return jnp.clip(values, min=-reach, max=reach).astype(kind)


def setup_inputs(seed: int = 0) -> dict:
    key_of = jax.random.split(jax.random.key(seed), 8)
    return {
        "features": scatter_about(key_of[0], (C, NX, NY, NZ), 1.0, 6.0, ((1, 4), (2, 2), (3, 4))),
        "cotangent": scatter_about(key_of[1], (C, NX, NY, NZ), 1.0, 6.0, ((1, 4), (2, 2), (3, 4))),
        "w_fine_in": scatter_about(key_of[2], (27, C, C), (27 * C) ** -0.5, 0.21875),
        "w_coarse_in": scatter_about(key_of[3], (27, C, CC), (27 * C) ** -0.5, 0.21875),
        "w_coarse_mid": scatter_about(key_of[4], (27, CC, CC), (27 * CC) ** -0.5, 0.109375),
        "w_lift": scatter_about(key_of[5], (CC, C), CC ** -0.5, 0.5),
        "w_fine_out": scatter_about(key_of[6], (27, C, C), (27 * C) ** -0.5, 0.21875),
    }


def conv_full(field, weight):
    cin = weight.shape[1]
    cout = weight.shape[2]
    kernel = weight.astype(jnp.float32).reshape(3, 3, 3, cin, cout).transpose(4, 3, 0, 1, 2)
    result = lax.conv_general_dilated(field.astype(jnp.float32)[None], kernel, (1, 1, 1), [(1, 1), (1, 1), (1, 1)], dimension_numbers=('NCDHW', 'OIDHW', 'NCDHW'), precision=lax.Precision.HIGHEST)
    return result[0]

def conv_back(grad, weight):
    return conv_full(grad, jnp.flip(weight, 0).transpose(0, 2, 1))

def weight_grad(field, grad):
    cin = field.shape[0]
    cout = grad.shape[0]
    depth, height, length = (field.shape[1], field.shape[2], field.shape[3])
    padded = jnp.pad(field.astype(jnp.float32), ((0, 0), (1, 1), (1, 1), (1, 1)))
    flat_grad = grad.astype(jnp.float32).reshape(cout, -1)
    blocks = []
    for tap in range(27):
        shift_x, shift_y, shift_z = (tap // 9, tap // 3 % 3, tap % 3)
        window = padded[:, shift_x:shift_x + depth, shift_y:shift_y + height, shift_z:shift_z + length].reshape(cin, -1)
        blocks.append(lax.dot_general(window, flat_grad, (((1,), (1,)), ((), ())), precision=lax.Precision.HIGHEST))
    return jnp.stack(blocks)

def pool_blocks(field):
    chans, depth, height, length = field.shape
    grouped = field.astype(jnp.float32).reshape(chans, depth // 4, 4, height // 4, 4, length // 4, 4)
    return grouped.sum(axis=(2, 4, 6))

def spread_up(field):
    chans, depth, height, length = field.shape
    grown = jnp.broadcast_to(field[:, :, None, :, None, :, None], (chans, depth, 4, height, 4, length, 4))
    return grown.reshape(chans, depth * 4, height * 4, length * 4)

def silu_slope(values):
    sigma = jax.nn.sigmoid(values)
    return sigma * (1.0 + values * (1.0 - sigma))

def reference(features, cotangent, w_fine_in, w_coarse_in, w_coarse_mid, w_lift, w_fine_out):
    scale = 1.0 / math.sqrt(NX * NY * NZ)
    z_first = conv_full(features, w_fine_in)
    act_first = jax.nn.silu(z_first).astype(jnp.bfloat16)
    pooled = (pool_blocks(act_first) / 64.0).astype(jnp.bfloat16)
    z_second = conv_full(pooled, w_coarse_in)
    act_second = jax.nn.silu(z_second).astype(jnp.bfloat16)
    z_third = conv_full(act_second, w_coarse_mid)
    act_third = jax.nn.silu(z_third).astype(jnp.bfloat16)
    lift_f = w_lift.astype(jnp.float32)
    third_f = act_third.astype(jnp.float32)
    lifted = jnp.tensordot(lift_f, third_f, axes=((0,), (0,)), precision=lax.Precision.HIGHEST)
    joined = (act_first.astype(jnp.float32) + spread_up(lifted)).astype(jnp.bfloat16)
    output = conv_full(joined, w_fine_out).astype(jnp.bfloat16)
    grad_fine_out = weight_grad(joined, cotangent) * scale
    d_joined = conv_back(cotangent, w_fine_out)
    d_lift = pool_blocks(d_joined)
    grad_lift = jnp.tensordot(third_f, d_lift, axes=((1, 2, 3), (1, 2, 3)), precision=lax.Precision.HIGHEST) * scale
    d_third = jnp.tensordot(lift_f, d_lift, axes=((1,), (0,)), precision=lax.Precision.HIGHEST)
    dz_third = (d_third * silu_slope(z_third)).astype(jnp.bfloat16)
    grad_coarse_mid = weight_grad(act_second, dz_third) * scale
    dz_second = (conv_back(dz_third, w_coarse_mid) * silu_slope(z_second)).astype(jnp.bfloat16)
    grad_coarse_in = weight_grad(pooled, dz_second) * scale
    d_pool = conv_back(dz_second, w_coarse_in)
    dz_first = ((d_joined + spread_up(d_pool) / 64.0) * silu_slope(z_first)).astype(jnp.bfloat16)
    grad_fine_in = weight_grad(features, dz_first) * scale
    grad_input = conv_back(dz_first, w_fine_in).astype(jnp.bfloat16)
    return (output, grad_input, grad_fine_in, grad_coarse_in, grad_coarse_mid, grad_lift, grad_fine_out)
```

```python
import math

import jax
import jax.numpy as jnp
from jax import lax
from jax.experimental import pallas as pl
from jax.experimental.pallas import tpu as pltpu
from jax.sharding import PartitionSpec as P

AXES = ("gx", "gy", "gz")
MESH = pl.DeviceIdType.MESH
DIRECT = 64


def place(flat, counts):
    nx, ny, nz = counts
    return (flat // (ny * nz), (flat // nz) % ny, flat % nz)


def meet(counts, total, me):
    barrier = pltpu.get_barrier_semaphore()

    def greet(k, carry):
        pl.semaphore_signal(
            barrier, inc=1, device_id=place((me + k) % total, counts), device_id_type=MESH
        )
        return carry

    lax.fori_loop(1, total, greet, 0)
    pl.semaphore_wait(barrier, total - 1)


def spread_kernel(counts, each, x_ref, o_ref, local_sem, send_sem, recv_sem):
    total = counts[0] * counts[1] * counts[2]
    me = (lax.axis_index("gx") * counts[1] + lax.axis_index("gy")) * counts[2] + lax.axis_index(
        "gz"
    )
    meet(counts, total, me)

    def copy(k):
        peer = (me + k) % total
        return pltpu.make_async_remote_copy(
            src_ref=x_ref.at[peer] if each else x_ref,
            dst_ref=o_ref.at[me],
            send_sem=send_sem.at[k],
            recv_sem=recv_sem.at[k],
            device_id=place(peer, counts),
            device_id_type=MESH,
        )

    def begin(k, carry):
        copy(k).start()
        return carry

    def finish(k, carry):
        copy(k).wait()
        return carry

    lax.fori_loop(1, total, begin, 0)
    own = pltpu.make_async_copy(x_ref.at[me] if each else x_ref, o_ref.at[me], local_sem)
    own.start()
    own.wait()
    lax.fori_loop(1, total, finish, 0)


def spread(x, counts, each, ident):
    total = counts[0] * counts[1] * counts[2]
    block = x.shape[1:] if each else x.shape
    return pl.pallas_call(
        lambda *refs: spread_kernel(counts, each, *refs),
        out_shape=jax.ShapeDtypeStruct((total,) + block, x.dtype),
        in_specs=[pl.BlockSpec(memory_space=pltpu.VMEM)],
        out_specs=pl.BlockSpec(memory_space=pltpu.VMEM),
        scratch_shapes=[
            pltpu.SemaphoreType.DMA,
            pltpu.SemaphoreType.DMA((total,)),
            pltpu.SemaphoreType.DMA((total,)),
        ],
        compiler_params=pltpu.CompilerParams(collective_id=ident, has_side_effects=True),
        name="spread_each" if each else "spread_all",
    )(x)


def extended(cells, sides, width):
    for axis, dim in sides:
        count = lax.axis_size(axis)
        ends = count - 1
        head = lax.slice_in_dim(cells, 0, width, axis=dim)
        tail = lax.slice_in_dim(cells, cells.shape[dim] - width, cells.shape[dim], axis=dim)
        cells = jnp.concatenate(
            [
                lax.ppermute(tail, axis, [(i, (i + 1) % count) for i in range(ends)]),
                cells,
                lax.ppermute(head, axis, [((i + 1) % count, i) for i in range(ends)]),
            ],
            axis=dim,
        )
    return cells


def silu_slope(values):
    sigma = jax.nn.sigmoid(values)
    return sigma * (1.0 + values * (1.0 - sigma))


def conv_valid(padded, weight, form="NCDHW"):
    kernel = weight.reshape(3, 3, 3, weight.shape[1], weight.shape[2])
    result = lax.conv_general_dilated(
        padded[None],
        kernel,
        (1, 1, 1),
        "VALID",
        dimension_numbers=(form, "DHWIO", form),
        preferred_element_type=jnp.float32,
    )
    return result[0]


def flipped(weight):
    return jnp.flip(weight, 0).transpose(0, 2, 1)


def windows_first(padded):
    chans, depth, height, length = padded.shape
    depth, height, length = depth - 2, height - 2, length - 2
    return jnp.stack(
        [
            padded[:, t // 9 : t // 9 + depth, t // 3 % 3 : t // 3 % 3 + height, t % 3 : t % 3 + length]
            for t in range(27)
        ]
    ).reshape(27 * chans, depth * height * length)


def pool_blocks(field):
    chans, depth, height, length = field.shape
    grouped = field.astype(jnp.float32).reshape(
        chans, depth // 4, 4, height // 4, 4, length // 4, 4
    )
    return grouped.sum(axis=(2, 4, 6))


def spread_up(field):
    chans, depth, height, length = field.shape
    grown = jnp.broadcast_to(
        field[:, :, None, :, None, :, None], (chans, depth, 4, height, 4, length, 4)
    )
    return grown.reshape(chans, depth * 4, height * 4, length * 4)


def inside(axis, size):
    at = lax.axis_index(axis) * size + jnp.arange(-1, size + 1)
    return (at >= 0) & (at < size * lax.axis_size(axis))


def rim(field, width=1):
    return jnp.pad(field, ((width, width),) * 3 + ((0, 0),))


def tap_grad_direct(padded, grad):
    depth = padded.shape[1] - 2
    height = padded.shape[2] - 2
    length = padded.shape[3] - 2
    flat_grad = grad.reshape(grad.shape[0], -1)
    blocks = []
    for tap in range(27):
        shift_x, shift_y, shift_z = (tap // 9, tap // 3 % 3, tap % 3)
        window = padded[
            :, shift_x : shift_x + depth, shift_y : shift_y + height, shift_z : shift_z + length
        ].reshape(padded.shape[0], -1)
        blocks.append(
            lax.dot_general(
                window, flat_grad, (((1,), (1,)), ((), ())), preferred_element_type=jnp.float32
            )
        )
    return jnp.stack(blocks)


def fine_rim(field):
    return extended(field, (("gx", 1), ("gy", 2), ("gz", 3)), 1)


def coarse_rim(field):
    return extended(field, (("gx", 1), ("gy", 2), ("gz", 3)), 1)


def reduce_grad(partial_value):
    first = lax.psum_scatter(partial_value, "gx", scatter_dimension=1, tiled=True)
    return lax.psum_scatter(first, ("gy", "gz"), scatter_dimension=2, tiled=True)


def input_share(field):
    parts = lax.all_to_all(field[None], "gx", split_axis=1, concat_axis=0, tiled=True)
    moved = jnp.moveaxis(parts, 0, 1)
    moved = moved.reshape(moved.shape[0], -1, moved.shape[3], moved.shape[4])
    moved = lax.all_gather(moved, "gy", axis=2, tiled=True)
    return lax.all_gather(moved, "gz", axis=3, tiled=True)


def output_share(field):
    parts = lax.all_to_all(field[None], ("gy", "gz"), split_axis=1, concat_axis=0, tiled=True)
    count_y = lax.axis_size("gy")
    count_z = lax.axis_size("gz")
    chans = parts.shape[1]
    depth, height, length = (parts.shape[2], parts.shape[3], parts.shape[4])
    grid = parts.reshape(count_y, count_z, chans, depth, height, length).transpose(2, 3, 0, 4, 1, 5)
    grid = grid.reshape(chans, depth, count_y * height, count_z * length)
    return lax.all_gather(grid, "gx", axis=1, tiled=True)


def shards_layered(features, cotangent, w_fine_in, w_coarse_in, w_coarse_mid, w_lift, w_fine_out):
    depth, height, length = (features.shape[1], features.shape[2], features.shape[3])
    whole_cells = (
        depth * lax.axis_size("gx") * height * lax.axis_size("gy") * length * lax.axis_size("gz")
    )
    scale = 1.0 / math.sqrt(whole_cells)
    padded_in = fine_rim(features)
    z_first = conv_valid(padded_in, w_fine_in)
    act_first = jax.nn.silu(z_first).astype(jnp.bfloat16)
    pooled = (pool_blocks(act_first) / 64.0).astype(jnp.bfloat16)
    pooled_pad = coarse_rim(pooled)
    z_second = conv_valid(pooled_pad, w_coarse_in)
    act_second = jax.nn.silu(z_second).astype(jnp.bfloat16)
    second_pad = coarse_rim(act_second)
    z_third = conv_valid(second_pad, w_coarse_mid)
    act_third = jax.nn.silu(z_third).astype(jnp.bfloat16)
    lifted = lax.dot_general(
        w_lift, act_third, (((0,), (0,)), ((), ())), preferred_element_type=jnp.float32
    )
    joined = (act_first.astype(jnp.float32) + spread_up(lifted)).astype(jnp.bfloat16)
    padded_joined = fine_rim(joined)
    output = conv_valid(padded_joined, w_fine_out).astype(jnp.bfloat16)
    part_fine_out = tap_grad_direct(padded_joined, cotangent) * scale
    d_joined = conv_valid(fine_rim(cotangent), flipped(w_fine_out))
    d_lift = pool_blocks(d_joined)
    lift_partial = (
        lax.dot_general(
            act_third.astype(jnp.float32),
            d_lift,
            (((1, 2, 3), (1, 2, 3)), ((), ())),
            precision=lax.Precision.HIGHEST,
        )
        * scale
    )
    d_third = lax.dot_general(
        w_lift.astype(jnp.float32),
        d_lift,
        (((1,), (0,)), ((), ())),
        precision=lax.Precision.HIGHEST,
    )
    dz_third = (d_third * silu_slope(z_third)).astype(jnp.bfloat16)
    dz_third_pad = coarse_rim(dz_third)
    grad_coarse_mid = None
    sources = input_share(act_second)
    sources_pad = jnp.pad(sources, ((0, 0), (1, 1), (1, 1), (1, 1)))
    targets = output_share(dz_third)
    grad_coarse_mid = tap_grad_direct(sources_pad, targets) * scale
    dz_second = (conv_valid(dz_third_pad, flipped(w_coarse_mid)) * silu_slope(z_second)).astype(
        jnp.bfloat16
    )
    dz_second_pad = coarse_rim(dz_second)
    part_coarse_in = tap_grad_direct(pooled_pad, dz_second) * scale
    d_pool = conv_valid(dz_second_pad, flipped(w_coarse_in))
    dz_first = ((d_joined + spread_up(d_pool) / 64.0) * silu_slope(z_first)).astype(jnp.bfloat16)
    part_fine_in = tap_grad_direct(padded_in, dz_first) * scale
    grad_input = conv_valid(fine_rim(dz_first), flipped(w_fine_in)).astype(jnp.bfloat16)
    pending = [part_fine_out, lift_partial[None], part_coarse_in, part_fine_in]
    reduced = [reduce_grad(partial_value) for partial_value in pending]
    grad_fine_out = reduced[0]
    grad_lift = reduced[1][0]
    grad_coarse_in = reduced[2]
    grad_fine_in = reduced[3]
    return (
        output,
        grad_input,
        grad_fine_in,
        grad_coarse_in,
        grad_coarse_mid,
        grad_lift,
        grad_fine_out,
    )


def shards(features, cotangent, w_fine_in, w_coarse_in, w_coarse_mid, w_lift, w_fine_out):
    counts = tuple(lax.axis_size(axis) for axis in AXES)
    nx, ny, nz = counts
    total = nx * ny * nz
    at_x, at_y, at_z = (lax.axis_index(axis) for axis in AXES)
    chans, depth, height, length = features.shape
    wide = w_lift.shape[0]
    cx, cy, cz = depth // 4, height // 4, length // 4
    scale = 1.0 / math.sqrt(total * depth * height * length)
    own = (slice(None),) + (slice(1, -1),) * 3

    both = extended(
        jnp.concatenate([features, cotangent]), (("gx", 1), ("gy", 2), ("gz", 3)), 2
    )
    z_first = conv_valid(both[:chans], w_fine_in)
    d_joined = conv_valid(both[chans:], flipped(w_fine_out))
    mask = (
        inside("gx", depth)[:, None, None]
        & inside("gy", height)[:, None]
        & inside("gz", length)
    )
    act_first = jnp.where(mask, jax.nn.silu(z_first), 0.0).astype(jnp.bfloat16)
    pooled = (pool_blocks(act_first[own]) / 64.0).astype(jnp.bfloat16)
    mine = jnp.concatenate([pooled.astype(jnp.float32), pool_blocks(d_joined[own])])
    mine = mine.reshape(2 * chans, cx * cy * cz).T

    full = spread(mine, counts, False, 0)
    full = full.reshape(nx, ny, nz, cx, cy, cz, 2 * chans)
    full = full.transpose(0, 3, 1, 4, 2, 5, 6).reshape(nx * cx, ny * cy, nz * cz, 2 * chans)
    pooled_full = full[..., :chans].astype(jnp.bfloat16)
    d_lift = full[..., chans:]
    grid = d_lift.shape[:3]
    cells = grid[0] * grid[1] * grid[2]

    z_second = conv_valid(rim(pooled_full), w_coarse_in, "NDHWC")
    act_second = jax.nn.silu(z_second).astype(jnp.bfloat16)
    z_third = conv_valid(rim(act_second), w_coarse_mid, "NDHWC")
    act_third = jax.nn.silu(z_third).astype(jnp.bfloat16)
    lifted = jnp.dot(act_third, w_lift, preferred_element_type=jnp.float32)
    d_third = lax.dot_general(
        d_lift,
        w_lift.astype(jnp.float32),
        (((3,), (1,)), ((), ())),
        precision=lax.Precision.HIGHEST,
    )
    dz_third = (d_third * silu_slope(z_third)).astype(jnp.bfloat16)
    dz_second = (
        conv_valid(rim(dz_third), flipped(w_coarse_mid), "NDHWC") * silu_slope(z_second)
    ).astype(jnp.bfloat16)

    at_o = at_y * nz + at_z

    def share(field, index, parts):
        size = field.shape[-1] // parts
        return lax.dynamic_slice_in_dim(field, index * size, size, axis=field.ndim - 1)

    def coarse_grad(field, grad):
        sources = share(field, at_x, nx).transpose(3, 0, 1, 2)
        sources = windows_first(jnp.pad(sources, ((0, 0),) + ((1, 1),) * 3))
        targets = share(grad, at_o, ny * nz).reshape(cells, -1)
        result = jnp.dot(sources, targets, preferred_element_type=jnp.float32)
        return result.reshape(27, -1, result.shape[-1]) * scale

    grad_coarse_mid = coarse_grad(act_second, dz_third)
    grad_coarse_in = coarse_grad(pooled_full, dz_second)
    grad_lift = (
        lax.dot_general(
            share(act_third, at_x, nx).reshape(cells, -1).astype(jnp.float32),
            share(d_lift, at_o, ny * nz).reshape(cells, -1),
            (((0,), (0,)), ((), ())),
            precision=lax.Precision.HIGHEST,
        )
        * scale
    )

    def local(field, width):
        return lax.dynamic_slice(
            rim(field, width),
            (at_x * cx, at_y * cy, at_z * cz, 0),
            (cx + 2 * width, cy + 2 * width, cz + 2 * width, field.shape[-1]),
        )

    def raised(field):
        return spread_up(field.transpose(3, 0, 1, 2))[:, 3:-3, 3:-3, 3:-3]

    joined = jnp.where(
        mask, act_first.astype(jnp.float32) + raised(local(lifted, 1)), 0.0
    ).astype(jnp.bfloat16)
    output = conv_valid(joined, w_fine_out).astype(jnp.bfloat16)
    d_pool = conv_valid(local(dz_second, 2), flipped(w_coarse_in), "NDHWC")
    dz_first = jnp.where(
        mask, (d_joined + raised(d_pool) / 64.0) * silu_slope(z_first), 0.0
    ).astype(jnp.bfloat16)
    grad_input = conv_valid(dz_first, flipped(w_fine_in)).astype(jnp.bfloat16)

    def fine_grad(field, grad):
        return lax.dot_general(
            grad.reshape(chans, -1),
            windows_first(field),
            (((1,), (1,)), ((), ())),
            preferred_element_type=jnp.float32,
        )

    parts = jnp.stack(
        [fine_grad(joined, cotangent), fine_grad(both[(slice(0, chans),) + (slice(1, -1),) * 3], dz_first[own])]
    )
    ci, co = chans // nx, chans // (ny * nz)
    parts = parts.reshape(2, ny * nz, co, 27, nx, ci).transpose(4, 1, 0, 2, 3, 5)
    parts = parts.reshape(total, 2 * co, 27 * ci)
    sums = spread(parts, counts, True, 1).sum(0) * scale
    sums = sums.reshape(2, co, 27, ci).transpose(0, 2, 3, 1)
    return (
        output,
        grad_input,
        sums[1],
        grad_coarse_in,
        grad_coarse_mid,
        grad_lift,
        sums[0],
    )


def choose(features, *rest):
    counts = [lax.axis_size(axis) for axis in AXES]
    coarse = math.prod(counts) * math.prod(features.shape[1:]) // 64
    whole = coarse <= 4096 and math.prod(counts) <= DIRECT
    return (shards if whole else shards_layered)(features, *rest)


def solution(mesh):
    whole = P(None, "gx", "gy", "gz")
    split = P(None, "gx", ("gy", "gz"))
    return jax.shard_map(
        choose,
        mesh=mesh,
        in_specs=(whole, whole, P(), P(), P(), P(), P()),
        out_specs=(whole, whole, split, split, split, P("gx", ("gy", "gz")), split),
        check_vma=False,
    )
```

```python
import math

import jax
import jax.numpy as jnp
from jax import lax
from jax.experimental import pallas as pl
from jax.experimental.pallas import tpu as pltpu
from jax.sharding import PartitionSpec as P

AXES = ("gx", "gy", "gz")
MESH = pl.DeviceIdType.MESH
DIRECT = 64


def place(flat, counts):
    nx, ny, nz = counts
    return (flat // (ny * nz), (flat // nz) % ny, flat % nz)


def meet(counts, total, me):
    barrier = pltpu.get_barrier_semaphore()

    def greet(k, carry):
        pl.semaphore_signal(
            barrier, inc=1, device_id=place((me + k) % total, counts), device_id_type=MESH
        )
        return carry

    lax.fori_loop(1, total, greet, 0)
    pl.semaphore_wait(barrier, total - 1)


def spread_kernel(counts, each, x_ref, o_ref, local_sem, send_sem, recv_sem):
    total = counts[0] * counts[1] * counts[2]
    me = (lax.axis_index("gx") * counts[1] + lax.axis_index("gy")) * counts[2] + lax.axis_index(
        "gz"
    )
    meet(counts, total, me)

    def copy(k):
        peer = (me + k) % total
        return pltpu.make_async_remote_copy(
            src_ref=x_ref.at[peer] if each else x_ref,
            dst_ref=o_ref.at[me],
            send_sem=send_sem.at[k],
            recv_sem=recv_sem.at[k],
            device_id=place(peer, counts),
            device_id_type=MESH,
        )

    def begin(k, carry):
        copy(k).start()
        return carry

    def finish(k, carry):
        copy(k).wait()
        return carry

    lax.fori_loop(1, total, begin, 0)
    own = pltpu.make_async_copy(x_ref.at[me] if each else x_ref, o_ref.at[me], local_sem)
    own.start()
    own.wait()
    lax.fori_loop(1, total, finish, 0)


def spread(x, counts, each, ident):
    total = counts[0] * counts[1] * counts[2]
    block = x.shape[1:] if each else x.shape
    return pl.pallas_call(
        lambda *refs: spread_kernel(counts, each, *refs),
        out_shape=jax.ShapeDtypeStruct((total,) + block, x.dtype),
        in_specs=[pl.BlockSpec(memory_space=pltpu.VMEM)],
        out_specs=pl.BlockSpec(memory_space=pltpu.VMEM),
        scratch_shapes=[
            pltpu.SemaphoreType.DMA,
            pltpu.SemaphoreType.DMA((total,)),
            pltpu.SemaphoreType.DMA((total,)),
        ],
        compiler_params=pltpu.CompilerParams(collective_id=ident, has_side_effects=True),
        name="spread_each" if each else "spread_all",
    )(x)


def extended(cells, sides, width):
    for axis, dim in sides:
        count = lax.axis_size(axis)
        ends = count - 1
        head = lax.slice_in_dim(cells, 0, width, axis=dim)
        tail = lax.slice_in_dim(cells, cells.shape[dim] - width, cells.shape[dim], axis=dim)
        cells = jnp.concatenate(
            [
                lax.ppermute(tail, axis, [(i, (i + 1) % count) for i in range(ends)]),
                cells,
                lax.ppermute(head, axis, [((i + 1) % count, i) for i in range(ends)]),
            ],
            axis=dim,
        )
    return cells


def silu_slope(values):
    sigma = jax.nn.sigmoid(values)
    return sigma * (1.0 + values * (1.0 - sigma))


def conv_valid(padded, weight, form="NCDHW"):
    kernel = weight.reshape(3, 3, 3, weight.shape[1], weight.shape[2])
    result = lax.conv_general_dilated(
        padded[None],
        kernel,
        (1, 1, 1),
        "VALID",
        dimension_numbers=(form, "DHWIO", form),
        preferred_element_type=jnp.float32,
    )
    return result[0]


def flipped(weight):
    return jnp.flip(weight, 0).transpose(0, 2, 1)


def pool_blocks(field):
    chans, depth, height, length = field.shape
    grouped = field.astype(jnp.float32).reshape(
        chans, depth // 4, 4, height // 4, 4, length // 4, 4
    )
    return grouped.sum(axis=(2, 4, 6))


def spread_up(field):
    chans, depth, height, length = field.shape
    grown = jnp.broadcast_to(
        field[:, :, None, :, None, :, None], (chans, depth, 4, height, 4, length, 4)
    )
    return grown.reshape(chans, depth * 4, height * 4, length * 4)


def tap_grad_direct(padded, grad):
    depth = padded.shape[1] - 2
    height = padded.shape[2] - 2
    length = padded.shape[3] - 2
    flat_grad = grad.reshape(grad.shape[0], -1)
    blocks = []
    for tap in range(27):
        shift_x, shift_y, shift_z = (tap // 9, tap // 3 % 3, tap % 3)
        window = padded[
            :, shift_x : shift_x + depth, shift_y : shift_y + height, shift_z : shift_z + length
        ].reshape(padded.shape[0], -1)
        blocks.append(
            lax.dot_general(
                window, flat_grad, (((1,), (1,)), ((), ())), preferred_element_type=jnp.float32
            )
        )
    return jnp.stack(blocks)


def fine_rim(field):
    return extended(field, (("gx", 1), ("gy", 2), ("gz", 3)), 1)


def coarse_rim(field):
    return extended(field, (("gx", 1), ("gy", 2), ("gz", 3)), 1)


def reduce_grad(partial_value):
    first = lax.psum_scatter(partial_value, "gx", scatter_dimension=1, tiled=True)
    return lax.psum_scatter(first, ("gy", "gz"), scatter_dimension=2, tiled=True)


def input_share(field):
    parts = lax.all_to_all(field[None], "gx", split_axis=1, concat_axis=0, tiled=True)
    moved = jnp.moveaxis(parts, 0, 1)
    moved = moved.reshape(moved.shape[0], -1, moved.shape[3], moved.shape[4])
    moved = lax.all_gather(moved, "gy", axis=2, tiled=True)
    return lax.all_gather(moved, "gz", axis=3, tiled=True)


def output_share(field):
    parts = lax.all_to_all(field[None], ("gy", "gz"), split_axis=1, concat_axis=0, tiled=True)
    count_y = lax.axis_size("gy")
    count_z = lax.axis_size("gz")
    chans = parts.shape[1]
    depth, height, length = (parts.shape[2], parts.shape[3], parts.shape[4])
    grid = parts.reshape(count_y, count_z, chans, depth, height, length).transpose(2, 3, 0, 4, 1, 5)
    grid = grid.reshape(chans, depth, count_y * height, count_z * length)
    return lax.all_gather(grid, "gx", axis=1, tiled=True)


def shards_layered(features, cotangent, w_fine_in, w_coarse_in, w_coarse_mid, w_lift, w_fine_out):
    depth, height, length = (features.shape[1], features.shape[2], features.shape[3])
    whole_cells = (
        depth * lax.axis_size("gx") * height * lax.axis_size("gy") * length * lax.axis_size("gz")
    )
    scale = 1.0 / math.sqrt(whole_cells)
    padded_in = fine_rim(features)
    z_first = conv_valid(padded_in, w_fine_in)
    act_first = jax.nn.silu(z_first).astype(jnp.bfloat16)
    pooled = (pool_blocks(act_first) / 64.0).astype(jnp.bfloat16)
    pooled_pad = coarse_rim(pooled)
    z_second = conv_valid(pooled_pad, w_coarse_in)
    act_second = jax.nn.silu(z_second).astype(jnp.bfloat16)
    second_pad = coarse_rim(act_second)
    z_third = conv_valid(second_pad, w_coarse_mid)
    act_third = jax.nn.silu(z_third).astype(jnp.bfloat16)
    lifted = lax.dot_general(
        w_lift, act_third, (((0,), (0,)), ((), ())), preferred_element_type=jnp.float32
    )
    joined = (act_first.astype(jnp.float32) + spread_up(lifted)).astype(jnp.bfloat16)
    padded_joined = fine_rim(joined)
    output = conv_valid(padded_joined, w_fine_out).astype(jnp.bfloat16)
    part_fine_out = tap_grad_direct(padded_joined, cotangent) * scale
    d_joined = conv_valid(fine_rim(cotangent), flipped(w_fine_out))
    d_lift = pool_blocks(d_joined)
    lift_partial = (
        lax.dot_general(
            act_third.astype(jnp.float32),
            d_lift,
            (((1, 2, 3), (1, 2, 3)), ((), ())),
            precision=lax.Precision.HIGHEST,
        )
        * scale
    )
    d_third = lax.dot_general(
        w_lift.astype(jnp.float32),
        d_lift,
        (((1,), (0,)), ((), ())),
        precision=lax.Precision.HIGHEST,
    )
    dz_third = (d_third * silu_slope(z_third)).astype(jnp.bfloat16)
    dz_third_pad = coarse_rim(dz_third)
    grad_coarse_mid = None
    sources = input_share(act_second)
    sources_pad = jnp.pad(sources, ((0, 0), (1, 1), (1, 1), (1, 1)))
    targets = output_share(dz_third)
    grad_coarse_mid = tap_grad_direct(sources_pad, targets) * scale
    dz_second = (conv_valid(dz_third_pad, flipped(w_coarse_mid)) * silu_slope(z_second)).astype(
        jnp.bfloat16
    )
    dz_second_pad = coarse_rim(dz_second)
    part_coarse_in = tap_grad_direct(pooled_pad, dz_second) * scale
    d_pool = conv_valid(dz_second_pad, flipped(w_coarse_in))
    dz_first = ((d_joined + spread_up(d_pool) / 64.0) * silu_slope(z_first)).astype(jnp.bfloat16)
    part_fine_in = tap_grad_direct(padded_in, dz_first) * scale
    grad_input = conv_valid(fine_rim(dz_first), flipped(w_fine_in)).astype(jnp.bfloat16)
    pending = [part_fine_out, lift_partial[None], part_coarse_in, part_fine_in]
    reduced = [reduce_grad(partial_value) for partial_value in pending]
    grad_fine_out = reduced[0]
    grad_lift = reduced[1][0]
    grad_coarse_in = reduced[2]
    grad_fine_in = reduced[3]
    return (
        output,
        grad_input,
        grad_fine_in,
        grad_coarse_in,
        grad_coarse_mid,
        grad_lift,
        grad_fine_out,
    )


def halo_kernel(counts, x_ref, o_ref, rows, packed, from_low, from_high, sends, recvs):
    nx, ny, nz = counts
    gx, gy, gz = (lax.axis_index(axis) for axis in AXES)
    sides = [(i, j, 0) for i in (-1, 0, 1) for j in (-1, 0, 1) if (i, j) != (0, 0)]
    sides += [(0, 0, -1), (0, 0, 1)]

    def there(side, sign):
        x, y, z = gx + sign * side[0], gy + sign * side[1], gz + sign * side[2]
        real = (x >= 0) & (x < nx) & (y >= 0) & (y < ny) & (z >= 0) & (z < nz)
        return (x, y, z), real

    rows[...] = jnp.zeros_like(rows)
    from_low[...] = jnp.zeros_like(from_low)
    from_high[...] = jnp.zeros_like(from_high)
    barrier = pltpu.get_barrier_semaphore()
    met = 0
    for side in sides:
        peer, real = there(side, 1)
        met = met + jnp.where(real, 1, 0)

        @pl.when(real)
        def _():
            pl.semaphore_signal(barrier, inc=1, device_id=peer, device_id_type=MESH)

    pl.semaphore_wait(barrier, met)
    d, h = x_ref.shape[:2]
    take = {-1: lambda n: pl.ds(0, 2), 0: lambda n: pl.ds(0, n), 1: lambda n: pl.ds(n - 2, 2)}
    land = {-1: lambda n: pl.ds(n + 2, 2), 0: lambda n: pl.ds(2, n), 1: lambda n: pl.ds(0, 2)}

    def transfer(k, side):
        if k < 8:
            source = x_ref.at[take[side[0]](d), take[side[1]](h)]
            target = rows.at[land[side[0]](d), land[side[1]](h)]
        else:
            source, target = packed, (from_high if side[2] < 0 else from_low)
        return pltpu.make_async_remote_copy(
            src_ref=source,
            dst_ref=target,
            send_sem=sends.at[k],
            recv_sem=recvs.at[k],
            device_id=there(side, 1)[0],
            device_id_type=MESH,
        )

    def run(first, last):
        for k in range(first, last):

            @pl.when(there(sides[k], 1)[1])
            def _():
                transfer(k, sides[k]).start()

    def settle(first, last):
        for k in range(first, last):

            @pl.when(there(sides[k], -1)[1])
            def _():
                transfer(k, sides[k]).wait_recv()

            @pl.when(there(sides[k], 1)[1])
            def _():
                transfer(k, sides[k]).wait_send()

    run(0, 8)
    settle(0, 8)
    rows[2 : 2 + d, 2 : 2 + h] = x_ref[...]
    lane = lax.broadcasted_iota(jnp.int32, (x_ref.shape[2], 128), 1)
    spots = [(x, y) for x in range(d + 4) for y in range(h + 4)]
    for part in range(2):
        group = jnp.zeros(lane.shape, jnp.float32)
        for r in range(32):
            x, y = spots[part * 32 + r]
            turned = pltpu.roll(rows[x, y].astype(jnp.float32), (2 + 4 * r) % 128, 1)
            group = jnp.where(lane // 4 == r, turned, group)
        packed[:, part * 128 : part * 128 + 128] = group.astype(jnp.bfloat16)
    run(8, 10)
    for x, y in spots:
        o_ref[x, y, :, 0:128] = rows[x, y]
    settle(8, 10)
    for part in range(2):
        span = slice(part * 128, part * 128 + 128)
        group = jnp.where(
            lane % 4 >= 2,
            from_high[:, span].astype(jnp.float32),
            from_low[:, span].astype(jnp.float32),
        )
        for r in range(32):
            x, y = spots[part * 32 + r]
            o_ref[x, y, :, 128:256] = pltpu.roll(group, 126 - 4 * r if r < 32 else 0, 1).astype(
                jnp.bfloat16
            )


def vmem(count):
    return [pl.BlockSpec(memory_space=pltpu.VMEM)] * count


ROOMY = 60 * 1024 * 1024


def halo(x, counts, ident):
    d, h, chans, length = x.shape
    edge = pltpu.VMEM((chans, 256), jnp.bfloat16)
    return pl.pallas_call(
        lambda *refs: halo_kernel(counts, *refs),
        out_shape=jax.ShapeDtypeStruct((d + 4, h + 4, chans, 256), x.dtype),
        in_specs=vmem(1),
        out_specs=vmem(1)[0],
        scratch_shapes=[
            pltpu.VMEM((d + 4, h + 4, chans, length), x.dtype),
            edge,
            edge,
            edge,
            pltpu.SemaphoreType.DMA((10,)),
            pltpu.SemaphoreType.DMA((10,)),
        ],
        compiler_params=pltpu.CompilerParams(
            collective_id=ident, has_side_effects=True, vmem_limit_bytes=ROOMY
        ),
        name="halo",
    )(x)


def stacked(value):
    size = value.shape[1]
    return jnp.concatenate(
        [pltpu.roll(value, 1, 1), value, pltpu.roll(value, size - 1, 1)]
    ).astype(jnp.bfloat16)


def around(ref, x, y, rows, lanes):
    return jnp.concatenate(
        [ref[x + a, y + b, rows, lanes] for a in range(3) for b in range(3)]
    )


def dot(a, b):
    return jnp.dot(a, b, preferred_element_type=jnp.float32)


def dot_over(a, b, dims, precision=None):
    return lax.dot_general(
        a, b, ((dims[:1], dims[1:]), ((), ())), precision=precision, preferred_element_type=jnp.float32
    )


def fine_kernel(ext, w_in, w_out_back, z_ref, d_ref, mine, taps, total):
    def fill(r, carry):
        x, y = r // 8, r % 8
        for f in range(2):
            value = ext[x, y, f * 32 : f * 32 + 32, :].astype(jnp.float32)
            taps[x, y, f * 96 : f * 96 + 96, :] = stacked(value)
        return carry

    lax.fori_loop(0, 64, fill, 0)
    total[...] = jnp.zeros_like(total)

    def body(r, carry):
        x, y = r // 6, r % 6
        z = dot(w_in[...], around(taps, x, y, slice(0, 96), slice(None)))
        d = dot(w_out_back[...], around(taps, x, y, slice(96, 192), slice(None)))
        z_ref[x, y] = z
        d_ref[x, y] = d
        act = jax.nn.silu(z[:, :128]).astype(jnp.bfloat16).astype(jnp.float32)
        own = jnp.where((x >= 1) & (x <= 4) & (y >= 1) & (y <= 4), 1.0, 0.0)
        total[...] += own * jnp.concatenate([act, d[:, :128]])
        return carry

    lax.fori_loop(0, 36, body, 0)
    row = lax.broadcasted_iota(jnp.int32, (32, 128), 0)
    lane = lax.broadcasted_iota(jnp.int32, (32, 128), 1)
    pick = jnp.where(lane // 4 == row, 1.0, 0.0)
    sums = dot_over(pick, total[...], (1, 1), lax.Precision.HIGHEST)
    both = jnp.concatenate([sums[:, :32] * (1.0 / 64.0), sums[:, 32:]], axis=1)
    mine[...] = jnp.concatenate([both[:16], both[16:]], axis=1).astype(jnp.bfloat16)


def coarse_kernel(
    counts, scale, full, w_in, w_mid, w_lift, w_lift_back, w_mid_back, w_in_back,
    pick_mid, pick_in, pick_o, pick_lift,
    grown, g_mid, g_in, g_lift,
    pad_in, pad_mid, pad_smid, pad_sin, table,
):
    nx, ny, nz = counts
    cells = nx * ny * 128
    gx, gy, gz = (lax.axis_index(axis) for axis in AXES)
    for pad in (pad_in, pad_mid, pad_smid, pad_sin):
        pad[...] = jnp.zeros_like(pad)

    def fill(pad, value):
        at = lax.broadcasted_iota(jnp.int32, value.shape, 0) % 128
        low = jnp.where(at == 0, 0.0, pltpu.roll(value, 1, 0))
        high = jnp.where(at == 127, 0.0, pltpu.roll(value, cells - 1, 0))
        wide = jnp.concatenate([low, value, high], axis=1).astype(jnp.bfloat16)
        pad[1 : nx + 1, 1 : ny + 1] = wide.reshape(nx, ny, 128, wide.shape[1])

    def window(pad, ab):
        a, b = ab // 3, ab % 3
        return pad[a : a + nx, b : b + ny].reshape(cells, pad.shape[3])

    def conv(pad, weight):
        result = dot(window(pad, 0), weight[0])
        for ab in range(1, 9):
            result = result + dot(window(pad, ab), weight[ab])
        return result

    def slope(v):
        sigma = jax.nn.sigmoid(v)
        return sigma * (1.0 + v * (1.0 - sigma))

    pieces = []
    for k in range(nx * ny):
        for z in range(nz):
            block = full[k * nz + z]
            pieces += [block[:, :64], block[:, 64:]]
    both = jnp.concatenate(pieces)
    pooled, d_lift = both[:, :32], both[:, 32:]
    fill(pad_in, pooled.astype(jnp.float32))
    z_second = conv(pad_in, w_in)
    act_second = jax.nn.silu(z_second)
    fill(pad_mid, act_second)
    z_third = conv(pad_mid, w_mid)
    act_third = jax.nn.silu(z_third).astype(jnp.bfloat16)
    lifted = dot(act_third, w_lift[...])
    dz_third = (dot(d_lift, w_lift_back[...]) * slope(z_third)).astype(jnp.bfloat16)
    fill(pad_mid, dz_third.astype(jnp.float32))
    dz_second = (conv(pad_mid, w_mid_back) * slope(z_second)).astype(jnp.bfloat16)
    fill(pad_mid, dz_second.astype(jnp.float32))
    d_pool = conv(pad_mid, w_in_back)

    table[...] = (
        jnp.concatenate([lifted, d_pool * (1.0 / 64.0)], axis=1)
        .astype(jnp.bfloat16)
        .reshape(nx, ny, 128, 64)
    )
    row = lax.broadcasted_iota(jnp.int32, (128, 256), 0)
    lane = lax.broadcasted_iota(jnp.int32, (128, 256), 1)
    cell = jnp.where(lane < 192, lane // 4, -1) + gz * 32
    grow = jnp.where(row == cell, 1.0, 0.0).astype(jnp.bfloat16)
    for i in range(3):
        for j in range(3):
            x = jnp.clip(gx + i - 1, 0, nx - 1)
            y = jnp.clip(gy + j - 1, 0, ny - 1)
            grown[i, j] = dot_over(table[x, y], grow, (0, 0))

    third_o = dot(dz_third, pick_o[...]).T.astype(jnp.bfloat16)
    second_o = dot(dz_second, pick_o[...]).T.astype(jnp.bfloat16)
    fill(pad_smid, dot(act_second.astype(jnp.bfloat16), pick_mid[...]))
    fill(pad_sin, dot(pooled, pick_in[...]))
    for ab in range(9):
        g_mid[ab] = dot(third_o, window(pad_smid, ab)) * scale
        g_in[ab] = dot(second_o, window(pad_sin, ab)) * scale
    third_i = dot(act_third, pick_mid[...]).astype(jnp.bfloat16)
    lift_o = dot(d_lift, pick_lift[...]).T.astype(jnp.bfloat16)
    g_lift[...] = dot(lift_o, third_i) * scale


def last_kernel(
    counts, ext, z_ref, d_ref, grown, w_out, w_in_back, out, g_input, parts, tj, td, tf, sums
):
    nx, ny, nz = counts
    gx, gy, gz = (lax.axis_index(axis) for axis in AXES)
    lane = lax.broadcasted_iota(jnp.int32, (32, 256), 1)
    at_z = gz * 128 + jnp.where(lane < 192, lane, lane - 256)
    keep_z = jnp.where((at_z >= 0) & (at_z < nz * 128), 1.0, 0.0)

    def fill(r, carry):
        x, y = r // 6, r % 6
        at_x, at_y = gx * 4 + x - 1, gy * 4 + y - 1
        real = (at_x >= 0) & (at_x < nx * 4) & (at_y >= 0) & (at_y < ny * 4)
        keep = keep_z * jnp.where(real, 1.0, 0.0)
        up = grown[(x + 3) // 4, (y + 3) // 4]
        z = z_ref[x, y]
        sigma = jax.nn.sigmoid(z)
        act = (z * sigma).astype(jnp.bfloat16).astype(jnp.float32)
        joined = (act + up[:32]).astype(jnp.bfloat16).astype(jnp.float32) * keep
        dz = (d_ref[x, y] + up[32:]) * (sigma * (1.0 + z * (1.0 - sigma))) * keep
        dz = dz.astype(jnp.bfloat16).astype(jnp.float32)
        tj[x, y] = stacked(joined)[:, :128]
        td[x, y] = stacked(dz)[:, :128]
        tf[x, y] = stacked(ext[x + 1, y + 1, 0:32, :].astype(jnp.float32))[:, :128]
        return carry

    lax.fori_loop(0, 36, fill, 0)
    sums[...] = jnp.zeros_like(sums)

    def body(r, carry):
        x, y = r // 2, (r % 2) * 2
        whole = slice(None)

        def pair(ref):
            return jnp.concatenate(
                [around(ref, x, y, whole, whole), around(ref, x, y + 1, whole, whole)], axis=1
            )

        near = pair(tj)
        result = dot(w_out[...], near).astype(jnp.bfloat16)
        out[x, y], out[x, y + 1] = result[:, :128], result[:, 128:]
        cot = jnp.concatenate(
            [ext[x + 2, y + 2, 32:64, 0:128], ext[x + 2, y + 3, 32:64, 0:128]], axis=1
        )
        sums[0] += dot_over(near, cot, (1, 1))
        result = dot(w_in_back[...], pair(td)).astype(jnp.bfloat16)
        g_input[x, y], g_input[x, y + 1] = result[:, :128], result[:, 128:]
        grad = jnp.concatenate(
            [td[x + 1, y + 1, 32:64, :], td[x + 1, y + 2, 32:64, :]], axis=1
        )
        sums[1] += dot_over(pair(tf), grad, (1, 1))
        return carry

    lax.fori_loop(0, 8, body, 0)
    ci, co = 32 // nx, 32 // (ny * nz)
    for f in range(2):
        value = sums[f].reshape(27, nx, ci, 32)
        for i in range(nx):
            block = value[:, i].reshape(27 * ci, 32).T
            for j in range(ny * nz):
                parts[i * ny * nz + j, f * co : f * co + co, 0 : 27 * ci] = block[
                    j * co : j * co + co
                ].astype(jnp.bfloat16)


def shards(features, cotangent, w_fine_in, w_coarse_in, w_coarse_mid, w_lift, w_fine_out):
    counts = tuple(lax.axis_size(axis) for axis in AXES)
    nx, ny, nz = counts
    total = nx * ny * nz
    at_x, at_y, at_z = (lax.axis_index(axis) for axis in AXES)
    chans, depth, height, length = features.shape
    wide = w_lift.shape[0]
    scale = 1.0 / math.sqrt(total * depth * height * length)
    f32, bf16 = jnp.float32, jnp.bfloat16
    shape = jax.ShapeDtypeStruct
    params = pltpu.CompilerParams(vmem_limit_bytes=ROOMY)

    def ahead(weight):
        return weight.transpose(2, 0, 1).reshape(weight.shape[2], -1)

    def back(weight):
        return jnp.flip(weight, 0).transpose(1, 0, 2).reshape(weight.shape[1], -1)

    rows = jnp.concatenate([features, cotangent]).transpose(1, 2, 0, 3)
    ext = halo(rows, counts, 2)
    field = shape((6, 6, chans, 256), f32)
    z_first, d_joined, mine = pl.pallas_call(
        fine_kernel,
        out_shape=(field, field, shape((16, 128), bf16)),
        in_specs=vmem(3),
        out_specs=vmem(3),
        scratch_shapes=[pltpu.VMEM((8, 8, 192, 256), bf16), pltpu.VMEM((64, 128), f32)],
        compiler_params=params,
        name="fine",
    )(ext, ahead(w_fine_in), back(w_fine_out))

    full = spread(mine, counts, False, 0)

    def pick(size, parts, index):
        each = size // parts
        return (jnp.arange(size)[:, None] == index * each + jnp.arange(each)).astype(bf16)

    at_o = at_y * nz + at_z
    co, cw = wide // (ny * nz), wide // nx
    ci = chans // nx
    pads = [3 * chans, 3 * wide, 3 * cw, 3 * ci]
    grown, g_mid, g_in, g_lift = pl.pallas_call(
        lambda *refs: coarse_kernel(counts, scale, *refs),
        out_shape=(
            shape((3, 3, 2 * chans, 256), f32),
            shape((9, co, 3 * cw), f32),
            shape((9, co, 3 * ci), f32),
            shape((chans // (ny * nz), cw), f32),
        ),
        in_specs=vmem(11),
        out_specs=vmem(4),
        scratch_shapes=[pltpu.VMEM((nx + 2, ny + 2, 128, k), bf16) for k in pads]
        + [pltpu.VMEM((nx, ny, 128, 2 * chans), bf16)],
        compiler_params=params,
        name="coarse",
    )(
        full,
        w_coarse_in.reshape(9, 3 * chans, wide),
        w_coarse_mid.reshape(9, 3 * wide, wide),
        w_lift,
        w_lift.T,
        flipped(w_coarse_mid).reshape(9, 3 * wide, wide),
        flipped(w_coarse_in).reshape(9, 3 * wide, chans),
        pick(wide, nx, at_x),
        pick(chans, nx, at_x),
        pick(wide, ny * nz, at_o),
        pick(chans, ny * nz, at_o),
    )

    near = pltpu.VMEM((6, 6, 3 * chans, 128), bf16)
    block = (2 * chans // (ny * nz), 27 * ci)
    output, grad_input, parts = pl.pallas_call(
        lambda *refs: last_kernel(counts, *refs),
        out_shape=(
            shape((4, 4, chans, 128), bf16),
            shape((4, 4, chans, 128), bf16),
            shape((total,) + block, bf16),
        ),
        in_specs=vmem(6),
        out_specs=vmem(3),
        scratch_shapes=[near, near, near, pltpu.VMEM((2, 27 * chans, chans), f32)],
        compiler_params=params,
        name="last",
    )(ext, z_first, d_joined, grown, ahead(w_fine_out), back(w_fine_in))

    sums = spread(parts, counts, True, 1).astype(f32).sum(0) * scale
    sums = sums.reshape(2, -1, 27, ci).transpose(0, 2, 3, 1)

    def owned(grad):
        return grad.reshape(9, grad.shape[1], 3, -1).transpose(0, 2, 3, 1).reshape(
            27, -1, grad.shape[1]
        )

    return (
        output.transpose(2, 0, 1, 3),
        grad_input.transpose(2, 0, 1, 3),
        sums[1],
        owned(g_in),
        owned(g_mid),
        g_lift.T,
        sums[0],
    )


def choose(features, *rest):
    nx, ny, nz = (lax.axis_size(axis) for axis in AXES)
    total = nx * ny * nz
    wide = rest[4].shape[0]
    fits = features.shape == (32, 4, 4, 128) and nz == 4 and total <= DIRECT
    fits = fits and 32 % (ny * nz) == 0 and 32 % nx == 0 and 32 // nx == 8 and wide == 128
    return (shards if fits else shards_layered)(features, *rest)


def solution(mesh):
    whole = P(None, "gx", "gy", "gz")
    split = P(None, "gx", ("gy", "gz"))
    return jax.shard_map(
        choose,
        mesh=mesh,
        in_specs=(whole, whole, P(), P(), P(), P(), P()),
        out_specs=(whole, whole, split, split, split, P("gx", ("gy", "gz")), split),
        check_vma=False,
    )
```

```python
import math

import jax
import jax.numpy as jnp
from jax import lax
from jax.experimental import pallas as pl
from jax.experimental.pallas import tpu as pltpu
from jax.sharding import PartitionSpec as P

AXES = ("gx", "gy", "gz")
MESH = pl.DeviceIdType.MESH
DIRECT = 64


def place(flat, counts):
    nx, ny, nz = counts
    return (flat // (ny * nz), (flat // nz) % ny, flat % nz)


def meet(counts, total, me):
    barrier = pltpu.get_barrier_semaphore()

    def greet(k, carry):
        pl.semaphore_signal(
            barrier, inc=1, device_id=place((me + k) % total, counts), device_id_type=MESH
        )
        return carry

    lax.fori_loop(1, total, greet, 0)
    pl.semaphore_wait(barrier, total - 1)


def spread_kernel(counts, each, x_ref, o_ref, local_sem, send_sem, recv_sem, during):
    total = counts[0] * counts[1] * counts[2]
    me = (lax.axis_index("gx") * counts[1] + lax.axis_index("gy")) * counts[2] + lax.axis_index(
        "gz"
    )
    meet(counts, total, me)

    def copy(k):
        peer = (me + k) % total
        return pltpu.make_async_remote_copy(
            src_ref=x_ref.at[peer] if each else x_ref,
            dst_ref=o_ref.at[me],
            send_sem=send_sem.at[k],
            recv_sem=recv_sem.at[k],
            device_id=place(peer, counts),
            device_id_type=MESH,
        )

    def begin(k, carry):
        copy(k).start()
        return carry

    def finish(k, carry):
        copy(k).wait()
        return carry

    lax.fori_loop(1, total, begin, 0)
    own = pltpu.make_async_copy(x_ref.at[me] if each else x_ref, o_ref.at[me], local_sem)
    own.start()
    during()
    own.wait()
    lax.fori_loop(1, total, finish, 0)


def gather_kernel(counts, x_ref, w_mid, w_in, o_ref, mid_back, in_back, *sems):
    wide, narrow = w_mid.shape[2], in_back.shape[2]

    def turn():
        def body(ab, carry):
            for c in range(3):
                rows = slice(c * wide, c * wide + wide)
                mid_back[ab, rows, :] = w_mid[8 - ab, (2 - c) * wide : (3 - c) * wide, :].T
                in_back[ab, rows, :] = w_in[8 - ab, (2 - c) * narrow : (3 - c) * narrow, :].T
            return carry

        lax.fori_loop(0, 9, body, 0)

    spread_kernel(counts, False, x_ref, o_ref, *sems, turn)


def sum_kernel(counts, scale, x_ref, o_ref, landed, *sems):
    spread_kernel(counts, True, x_ref, landed, *sems, lambda: None)
    o_ref[...] = landed[...].astype(jnp.float32).sum(0) * scale


def spread_call(kernel, counts, ident, outs, scratch, name, *args):
    total = counts[0] * counts[1] * counts[2]
    return pl.pallas_call(
        kernel,
        out_shape=outs,
        in_specs=vmem(len(args)),
        out_specs=vmem(len(outs)),
        scratch_shapes=scratch
        + [
            pltpu.SemaphoreType.DMA,
            pltpu.SemaphoreType.DMA((total,)),
            pltpu.SemaphoreType.DMA((total,)),
        ],
        compiler_params=pltpu.CompilerParams(collective_id=ident, has_side_effects=True),
        name=name,
    )(*args)


def extended(cells, sides, width):
    for axis, dim in sides:
        count = lax.axis_size(axis)
        ends = count - 1
        head = lax.slice_in_dim(cells, 0, width, axis=dim)
        tail = lax.slice_in_dim(cells, cells.shape[dim] - width, cells.shape[dim], axis=dim)
        cells = jnp.concatenate(
            [
                lax.ppermute(tail, axis, [(i, (i + 1) % count) for i in range(ends)]),
                cells,
                lax.ppermute(head, axis, [((i + 1) % count, i) for i in range(ends)]),
            ],
            axis=dim,
        )
    return cells


def silu_slope(values):
    sigma = jax.nn.sigmoid(values)
    return sigma * (1.0 + values * (1.0 - sigma))


def conv_valid(padded, weight, form="NCDHW"):
    kernel = weight.reshape(3, 3, 3, weight.shape[1], weight.shape[2])
    result = lax.conv_general_dilated(
        padded[None],
        kernel,
        (1, 1, 1),
        "VALID",
        dimension_numbers=(form, "DHWIO", form),
        preferred_element_type=jnp.float32,
    )
    return result[0]


def flipped(weight):
    return jnp.flip(weight, 0).transpose(0, 2, 1)


def pool_blocks(field):
    chans, depth, height, length = field.shape
    grouped = field.astype(jnp.float32).reshape(
        chans, depth // 4, 4, height // 4, 4, length // 4, 4
    )
    return grouped.sum(axis=(2, 4, 6))


def spread_up(field):
    chans, depth, height, length = field.shape
    grown = jnp.broadcast_to(
        field[:, :, None, :, None, :, None], (chans, depth, 4, height, 4, length, 4)
    )
    return grown.reshape(chans, depth * 4, height * 4, length * 4)


def tap_grad_direct(padded, grad):
    depth = padded.shape[1] - 2
    height = padded.shape[2] - 2
    length = padded.shape[3] - 2
    flat_grad = grad.reshape(grad.shape[0], -1)
    blocks = []
    for tap in range(27):
        shift_x, shift_y, shift_z = (tap // 9, tap // 3 % 3, tap % 3)
        window = padded[
            :, shift_x : shift_x + depth, shift_y : shift_y + height, shift_z : shift_z + length
        ].reshape(padded.shape[0], -1)
        blocks.append(
            lax.dot_general(
                window, flat_grad, (((1,), (1,)), ((), ())), preferred_element_type=jnp.float32
            )
        )
    return jnp.stack(blocks)


def fine_rim(field):
    return extended(field, (("gx", 1), ("gy", 2), ("gz", 3)), 1)


def coarse_rim(field):
    return extended(field, (("gx", 1), ("gy", 2), ("gz", 3)), 1)


def reduce_grad(partial_value):
    first = lax.psum_scatter(partial_value, "gx", scatter_dimension=1, tiled=True)
    return lax.psum_scatter(first, ("gy", "gz"), scatter_dimension=2, tiled=True)


def input_share(field):
    parts = lax.all_to_all(field[None], "gx", split_axis=1, concat_axis=0, tiled=True)
    moved = jnp.moveaxis(parts, 0, 1)
    moved = moved.reshape(moved.shape[0], -1, moved.shape[3], moved.shape[4])
    moved = lax.all_gather(moved, "gy", axis=2, tiled=True)
    return lax.all_gather(moved, "gz", axis=3, tiled=True)


def output_share(field):
    parts = lax.all_to_all(field[None], ("gy", "gz"), split_axis=1, concat_axis=0, tiled=True)
    count_y = lax.axis_size("gy")
    count_z = lax.axis_size("gz")
    chans = parts.shape[1]
    depth, height, length = (parts.shape[2], parts.shape[3], parts.shape[4])
    grid = parts.reshape(count_y, count_z, chans, depth, height, length).transpose(2, 3, 0, 4, 1, 5)
    grid = grid.reshape(chans, depth, count_y * height, count_z * length)
    return lax.all_gather(grid, "gx", axis=1, tiled=True)


def shards_layered(features, cotangent, w_fine_in, w_coarse_in, w_coarse_mid, w_lift, w_fine_out):
    depth, height, length = (features.shape[1], features.shape[2], features.shape[3])
    whole_cells = (
        depth * lax.axis_size("gx") * height * lax.axis_size("gy") * length * lax.axis_size("gz")
    )
    scale = 1.0 / math.sqrt(whole_cells)
    padded_in = fine_rim(features)
    z_first = conv_valid(padded_in, w_fine_in)
    act_first = jax.nn.silu(z_first).astype(jnp.bfloat16)
    pooled = (pool_blocks(act_first) / 64.0).astype(jnp.bfloat16)
    pooled_pad = coarse_rim(pooled)
    z_second = conv_valid(pooled_pad, w_coarse_in)
    act_second = jax.nn.silu(z_second).astype(jnp.bfloat16)
    second_pad = coarse_rim(act_second)
    z_third = conv_valid(second_pad, w_coarse_mid)
    act_third = jax.nn.silu(z_third).astype(jnp.bfloat16)
    lifted = lax.dot_general(
        w_lift, act_third, (((0,), (0,)), ((), ())), preferred_element_type=jnp.float32
    )
    joined = (act_first.astype(jnp.float32) + spread_up(lifted)).astype(jnp.bfloat16)
    padded_joined = fine_rim(joined)
    output = conv_valid(padded_joined, w_fine_out).astype(jnp.bfloat16)
    part_fine_out = tap_grad_direct(padded_joined, cotangent) * scale
    d_joined = conv_valid(fine_rim(cotangent), flipped(w_fine_out))
    d_lift = pool_blocks(d_joined)
    lift_partial = (
        lax.dot_general(
            act_third.astype(jnp.float32),
            d_lift,
            (((1, 2, 3), (1, 2, 3)), ((), ())),
            precision=lax.Precision.HIGHEST,
        )
        * scale
    )
    d_third = lax.dot_general(
        w_lift.astype(jnp.float32),
        d_lift,
        (((1,), (0,)), ((), ())),
        precision=lax.Precision.HIGHEST,
    )
    dz_third = (d_third * silu_slope(z_third)).astype(jnp.bfloat16)
    dz_third_pad = coarse_rim(dz_third)
    grad_coarse_mid = None
    sources = input_share(act_second)
    sources_pad = jnp.pad(sources, ((0, 0), (1, 1), (1, 1), (1, 1)))
    targets = output_share(dz_third)
    grad_coarse_mid = tap_grad_direct(sources_pad, targets) * scale
    dz_second = (conv_valid(dz_third_pad, flipped(w_coarse_mid)) * silu_slope(z_second)).astype(
        jnp.bfloat16
    )
    dz_second_pad = coarse_rim(dz_second)
    part_coarse_in = tap_grad_direct(pooled_pad, dz_second) * scale
    d_pool = conv_valid(dz_second_pad, flipped(w_coarse_in))
    dz_first = ((d_joined + spread_up(d_pool) / 64.0) * silu_slope(z_first)).astype(jnp.bfloat16)
    part_fine_in = tap_grad_direct(padded_in, dz_first) * scale
    grad_input = conv_valid(fine_rim(dz_first), flipped(w_fine_in)).astype(jnp.bfloat16)
    pending = [part_fine_out, lift_partial[None], part_coarse_in, part_fine_in]
    reduced = [reduce_grad(partial_value) for partial_value in pending]
    grad_fine_out = reduced[0]
    grad_lift = reduced[1][0]
    grad_coarse_in = reduced[2]
    grad_fine_in = reduced[3]
    return (
        output,
        grad_input,
        grad_fine_in,
        grad_coarse_in,
        grad_coarse_mid,
        grad_lift,
        grad_fine_out,
    )


def halo_kernel(counts, x_ref, o_ref, rows, packed, from_low, from_high, sends, recvs):
    nx, ny, nz = counts
    gx, gy, gz = (lax.axis_index(axis) for axis in AXES)
    sides = [(i, j, 0) for i in (-1, 0, 1) for j in (-1, 0, 1) if (i, j) != (0, 0)]
    sides += [(0, 0, -1), (0, 0, 1)]

    def there(side, sign):
        x, y, z = gx + sign * side[0], gy + sign * side[1], gz + sign * side[2]
        real = (x >= 0) & (x < nx) & (y >= 0) & (y < ny) & (z >= 0) & (z < nz)
        return (x, y, z), real

    rows[...] = jnp.zeros_like(rows)
    from_low[...] = jnp.zeros_like(from_low)
    from_high[...] = jnp.zeros_like(from_high)
    barrier = pltpu.get_barrier_semaphore()
    met = 0
    for side in sides:
        peer, real = there(side, 1)
        met = met + jnp.where(real, 1, 0)

        @pl.when(real)
        def _():
            pl.semaphore_signal(barrier, inc=1, device_id=peer, device_id_type=MESH)

    pl.semaphore_wait(barrier, met)
    d, h = x_ref.shape[:2]
    take = {-1: lambda n: pl.ds(0, 2), 0: lambda n: pl.ds(0, n), 1: lambda n: pl.ds(n - 2, 2)}
    land = {-1: lambda n: pl.ds(n + 2, 2), 0: lambda n: pl.ds(2, n), 1: lambda n: pl.ds(0, 2)}

    def transfer(k, side):
        if k < 8:
            source = x_ref.at[take[side[0]](d), take[side[1]](h)]
            target = rows.at[land[side[0]](d), land[side[1]](h)]
        else:
            source, target = packed, (from_high if side[2] < 0 else from_low)
        return pltpu.make_async_remote_copy(
            src_ref=source,
            dst_ref=target,
            send_sem=sends.at[k],
            recv_sem=recvs.at[k],
            device_id=there(side, 1)[0],
            device_id_type=MESH,
        )

    def run(first, last):
        for k in range(first, last):

            @pl.when(there(sides[k], 1)[1])
            def _():
                transfer(k, sides[k]).start()

    def settle(first, last):
        for k in range(first, last):

            @pl.when(there(sides[k], -1)[1])
            def _():
                transfer(k, sides[k]).wait_recv()

            @pl.when(there(sides[k], 1)[1])
            def _():
                transfer(k, sides[k]).wait_send()

    run(0, 8)
    settle(0, 8)
    rows[2 : 2 + d, 2 : 2 + h] = x_ref[...]
    lane = lax.broadcasted_iota(jnp.int32, (x_ref.shape[2], 128), 1)
    spots = [(x, y) for x in range(d + 4) for y in range(h + 4)]
    for part in range(2):
        group = jnp.zeros(lane.shape, jnp.float32)
        for r in range(32):
            x, y = spots[part * 32 + r]
            turned = pltpu.roll(rows[x, y].astype(jnp.float32), (2 + 4 * r) % 128, 1)
            group = jnp.where(lane // 4 == r, turned, group)
        packed[:, part * 128 : part * 128 + 128] = group.astype(jnp.bfloat16)
    run(8, 10)
    for x, y in spots:
        o_ref[x, y, :, 0:128] = rows[x, y]
    settle(8, 10)
    for part in range(2):
        span = slice(part * 128, part * 128 + 128)
        group = jnp.where(
            lane % 4 >= 2,
            from_high[:, span].astype(jnp.float32),
            from_low[:, span].astype(jnp.float32),
        )
        for r in range(32):
            x, y = spots[part * 32 + r]
            o_ref[x, y, :, 128:256] = pltpu.roll(group, 126 - 4 * r if r < 32 else 0, 1).astype(
                jnp.bfloat16
            )


def vmem(count):
    return [pl.BlockSpec(memory_space=pltpu.VMEM)] * count


ROOMY = 60 * 1024 * 1024


def halo(x, counts, ident):
    d, h, chans, length = x.shape
    edge = pltpu.VMEM((chans, 256), jnp.bfloat16)
    return pl.pallas_call(
        lambda *refs: halo_kernel(counts, *refs),
        out_shape=jax.ShapeDtypeStruct((d + 4, h + 4, chans, 256), x.dtype),
        in_specs=vmem(1),
        out_specs=vmem(1)[0],
        scratch_shapes=[
            pltpu.VMEM((d + 4, h + 4, chans, length), x.dtype),
            edge,
            edge,
            edge,
            pltpu.SemaphoreType.DMA((10,)),
            pltpu.SemaphoreType.DMA((10,)),
        ],
        compiler_params=pltpu.CompilerParams(
            collective_id=ident, has_side_effects=True, vmem_limit_bytes=ROOMY
        ),
        name="halo",
    )(x)


def stacked(value):
    size = value.shape[1]
    return jnp.concatenate(
        [pltpu.roll(value, 1, 1), value, pltpu.roll(value, size - 1, 1)]
    ).astype(jnp.bfloat16)


def around(ref, x, y, rows, lanes):
    return jnp.concatenate(
        [ref[x + a, y + b, rows, lanes] for a in range(3) for b in range(3)]
    )


def dot(a, b):
    return jnp.dot(a, b, preferred_element_type=jnp.float32)


def dot_over(a, b, dims, precision=None):
    return lax.dot_general(
        a, b, ((dims[:1], dims[1:]), ((), ())), precision=precision, preferred_element_type=jnp.float32
    )


def ahead(weight):
    return weight[...].reshape(27 * weight.shape[1], weight.shape[2]).T


def back(weight):
    return jnp.concatenate([weight[26 - t] for t in range(27)], axis=1)


def fine_kernel(ext, w_in, w_out, z_ref, d_ref, mine, taps, total, ws):
    ws[0], ws[1] = ahead(w_in), back(w_out)

    def fill(r, carry):
        x, y = r // 8, r % 8
        for f in range(2):
            value = ext[x, y, f * 32 : f * 32 + 32, :].astype(jnp.float32)
            taps[x, y, f * 96 : f * 96 + 96, :] = stacked(value)
        return carry

    lax.fori_loop(0, 64, fill, 0)
    total[...] = jnp.zeros_like(total)

    def body(r, carry):
        x, y = r // 6, r % 6
        z = dot(ws[0], around(taps, x, y, slice(0, 96), slice(None)))
        d = dot(ws[1], around(taps, x, y, slice(96, 192), slice(None)))
        z_ref[x, y] = z
        d_ref[x, y] = d
        act = jax.nn.silu(z[:, :128]).astype(jnp.bfloat16).astype(jnp.float32)
        own = jnp.where((x >= 1) & (x <= 4) & (y >= 1) & (y <= 4), 1.0, 0.0)
        total[...] += own * jnp.concatenate([act, d[:, :128]])
        return carry

    lax.fori_loop(0, 36, body, 0)
    row = lax.broadcasted_iota(jnp.int32, (32, 128), 0)
    lane = lax.broadcasted_iota(jnp.int32, (32, 128), 1)
    pick = jnp.where(lane // 4 == row, 1.0, 0.0)
    sums = dot_over(pick, total[...], (1, 1), lax.Precision.HIGHEST)
    both = jnp.concatenate([sums[:, :32] * (1.0 / 64.0), sums[:, 32:]], axis=1)
    mine[...] = jnp.concatenate([both[:16], both[16:]], axis=1).astype(jnp.bfloat16)


def coarse_kernel(
    counts, scale, full, w_in, w_mid, w_lift, w_mid_back, w_in_back,
    grown, g_mid, g_in, g_lift,
    pad_in, pad_mid, pad_smid, pad_sin, table,
):
    nx, ny, nz = counts
    cells = nx * ny * 128
    gx, gy, gz = (lax.axis_index(axis) for axis in AXES)
    for pad in (pad_in, pad_mid, pad_smid, pad_sin):
        pad[...] = jnp.zeros_like(pad)

    def pick(size, parts, index):
        each = size // parts
        row = lax.broadcasted_iota(jnp.int32, (size, each), 0)
        column = lax.broadcasted_iota(jnp.int32, (size, each), 1)
        return jnp.where(row == index * each + column, 1.0, 0.0).astype(jnp.bfloat16)

    at_o = gy * nz + gz
    pick_mid, pick_in = pick(128, nx, gx), pick(32, nx, gx)
    pick_o, pick_lift = pick(128, ny * nz, at_o), pick(32, ny * nz, at_o)

    def fill(pad, value):
        at = lax.broadcasted_iota(jnp.int32, value.shape, 0) % 128
        low = jnp.where(at == 0, 0.0, pltpu.roll(value, 1, 0))
        high = jnp.where(at == 127, 0.0, pltpu.roll(value, cells - 1, 0))
        wide = jnp.concatenate([low, value, high], axis=1).astype(jnp.bfloat16)
        pad[1 : nx + 1, 1 : ny + 1] = wide.reshape(nx, ny, 128, wide.shape[1])

    def window(pad, ab):
        a, b = ab // 3, ab % 3
        return pad[a : a + nx, b : b + ny].reshape(cells, pad.shape[3])

    def conv(pad, weight):
        result = dot(window(pad, 0), weight[0])
        for ab in range(1, 9):
            result = result + dot(window(pad, ab), weight[ab])
        return result

    def slope(v):
        sigma = jax.nn.sigmoid(v)
        return sigma * (1.0 + v * (1.0 - sigma))

    pieces = []
    for k in range(nx * ny):
        for z in range(nz):
            block = full[k * nz + z]
            pieces += [block[:, :64], block[:, 64:]]
    both = jnp.concatenate(pieces)
    pooled, d_lift = both[:, :32], both[:, 32:]
    fill(pad_in, pooled.astype(jnp.float32))
    z_second = conv(pad_in, w_in)
    act_second = jax.nn.silu(z_second)
    fill(pad_mid, act_second)
    z_third = conv(pad_mid, w_mid)
    act_third = jax.nn.silu(z_third).astype(jnp.bfloat16)
    lifted = dot(act_third, w_lift[...])
    dz_third = (dot_over(d_lift, w_lift[...], (1, 1)) * slope(z_third)).astype(jnp.bfloat16)
    fill(pad_mid, dz_third.astype(jnp.float32))
    dz_second = (conv(pad_mid, w_mid_back) * slope(z_second)).astype(jnp.bfloat16)
    fill(pad_mid, dz_second.astype(jnp.float32))
    d_pool = conv(pad_mid, w_in_back)

    table[...] = (
        jnp.concatenate([lifted, d_pool * (1.0 / 64.0)], axis=1)
        .astype(jnp.bfloat16)
        .reshape(nx, ny, 128, 64)
    )
    row = lax.broadcasted_iota(jnp.int32, (128, 256), 0)
    lane = lax.broadcasted_iota(jnp.int32, (128, 256), 1)
    cell = jnp.where(lane < 192, lane // 4, -1) + gz * 32
    grow = jnp.where(row == cell, 1.0, 0.0).astype(jnp.bfloat16)
    for i in range(3):
        for j in range(3):
            x = jnp.clip(gx + i - 1, 0, nx - 1)
            y = jnp.clip(gy + j - 1, 0, ny - 1)
            grown[i, j] = dot_over(table[x, y], grow, (0, 0))

    third_o = dot(dz_third, pick_o).T.astype(jnp.bfloat16)
    second_o = dot(dz_second, pick_o).T.astype(jnp.bfloat16)
    fill(pad_smid, dot(act_second.astype(jnp.bfloat16), pick_mid))
    fill(pad_sin, dot(pooled, pick_in))
    for ab in range(9):
        g_mid[ab] = dot(third_o, window(pad_smid, ab)) * scale
        g_in[ab] = dot(second_o, window(pad_sin, ab)) * scale
    third_i = dot(act_third, pick_mid).astype(jnp.bfloat16)
    lift_o = dot(d_lift, pick_lift).T.astype(jnp.bfloat16)
    g_lift[...] = dot(lift_o, third_i) * scale


def last_kernel(
    counts, ext, z_ref, d_ref, grown, w_out, w_in, out, g_input, parts, tj, td, tf, sums, ws
):
    ws[0], ws[1] = ahead(w_out), back(w_in)
    nx, ny, nz = counts
    gx, gy, gz = (lax.axis_index(axis) for axis in AXES)
    lane = lax.broadcasted_iota(jnp.int32, (32, 256), 1)
    at_z = gz * 128 + jnp.where(lane < 192, lane, lane - 256)
    keep_z = jnp.where((at_z >= 0) & (at_z < nz * 128), 1.0, 0.0)

    def fill(r, carry):
        x, y = r // 6, r % 6
        at_x, at_y = gx * 4 + x - 1, gy * 4 + y - 1
        real = (at_x >= 0) & (at_x < nx * 4) & (at_y >= 0) & (at_y < ny * 4)
        keep = keep_z * jnp.where(real, 1.0, 0.0)
        up = grown[(x + 3) // 4, (y + 3) // 4]
        z = z_ref[x, y]
        sigma = jax.nn.sigmoid(z)
        act = (z * sigma).astype(jnp.bfloat16).astype(jnp.float32)
        joined = (act + up[:32]).astype(jnp.bfloat16).astype(jnp.float32) * keep
        dz = (d_ref[x, y] + up[32:]) * (sigma * (1.0 + z * (1.0 - sigma))) * keep
        dz = dz.astype(jnp.bfloat16).astype(jnp.float32)
        tj[x, y] = stacked(joined)[:, :128]
        td[x, y] = stacked(dz)[:, :128]
        tf[x, y] = stacked(ext[x + 1, y + 1, 0:32, :].astype(jnp.float32))[:, :128]
        return carry

    lax.fori_loop(0, 36, fill, 0)
    sums[...] = jnp.zeros_like(sums)

    def body(r, carry):
        x, y = r // 2, (r % 2) * 2
        whole = slice(None)

        def pair(ref):
            return jnp.concatenate(
                [around(ref, x, y, whole, whole), around(ref, x, y + 1, whole, whole)], axis=1
            )

        near = pair(tj)
        result = dot(ws[0], near).astype(jnp.bfloat16)
        out[x, y], out[x, y + 1] = result[:, :128], result[:, 128:]
        cot = jnp.concatenate(
            [ext[x + 2, y + 2, 32:64, 0:128], ext[x + 2, y + 3, 32:64, 0:128]], axis=1
        )
        sums[0] += dot_over(near, cot, (1, 1))
        result = dot(ws[1], pair(td)).astype(jnp.bfloat16)
        g_input[x, y], g_input[x, y + 1] = result[:, :128], result[:, 128:]
        grad = jnp.concatenate(
            [td[x + 1, y + 1, 32:64, :], td[x + 1, y + 2, 32:64, :]], axis=1
        )
        sums[1] += dot_over(pair(tf), grad, (1, 1))
        return carry

    lax.fori_loop(0, 8, body, 0)
    ci, co = 32 // nx, 32 // (ny * nz)
    for f in range(2):
        value = sums[f].reshape(27, nx, ci, 32)
        for i in range(nx):
            block = value[:, i].reshape(27 * ci, 32).T
            for j in range(ny * nz):
                parts[i * ny * nz + j, f * co : f * co + co, 0 : 27 * ci] = block[
                    j * co : j * co + co
                ].astype(jnp.bfloat16)


def shards(features, cotangent, w_fine_in, w_coarse_in, w_coarse_mid, w_lift, w_fine_out):
    counts = tuple(lax.axis_size(axis) for axis in AXES)
    nx, ny, nz = counts
    total = nx * ny * nz
    chans, depth, height, length = features.shape
    wide = w_lift.shape[0]
    scale = 1.0 / math.sqrt(total * depth * height * length)
    f32, bf16 = jnp.float32, jnp.bfloat16
    shape = jax.ShapeDtypeStruct
    params = pltpu.CompilerParams(vmem_limit_bytes=ROOMY)

    rows = jnp.concatenate([features, cotangent]).transpose(1, 2, 0, 3)
    ext = halo(rows, counts, 2)
    field = shape((6, 6, chans, 256), f32)
    z_first, d_joined, mine = pl.pallas_call(
        fine_kernel,
        out_shape=(field, field, shape((16, 128), bf16)),
        in_specs=vmem(3),
        out_specs=vmem(3),
        scratch_shapes=[
            pltpu.VMEM((8, 8, 192, 256), bf16),
            pltpu.VMEM((64, 128), f32),
            pltpu.VMEM((2, chans, 27 * chans), bf16),
        ],
        compiler_params=params,
        name="fine",
    )(ext, w_fine_in, w_fine_out)

    w_in9 = w_coarse_in.reshape(9, 3 * chans, wide)
    w_mid9 = w_coarse_mid.reshape(9, 3 * wide, wide)
    full, mid_back, in_back = spread_call(
        lambda *refs: gather_kernel(counts, *refs),
        counts,
        0,
        (
            shape((total,) + mine.shape, bf16),
            shape(w_mid9.shape, bf16),
            shape((9, 3 * wide, chans), bf16),
        ),
        [],
        "gather",
        mine,
        w_mid9,
        w_in9,
    )

    co, cw = wide // (ny * nz), wide // nx
    ci = chans // nx
    pads = [3 * chans, 3 * wide, 3 * cw, 3 * ci]
    grown, g_mid, g_in, g_lift = pl.pallas_call(
        lambda *refs: coarse_kernel(counts, scale, *refs),
        out_shape=(
            shape((3, 3, 2 * chans, 256), f32),
            shape((9, co, 3 * cw), f32),
            shape((9, co, 3 * ci), f32),
            shape((chans // (ny * nz), cw), f32),
        ),
        in_specs=vmem(6),
        out_specs=vmem(4),
        scratch_shapes=[pltpu.VMEM((nx + 2, ny + 2, 128, k), bf16) for k in pads]
        + [pltpu.VMEM((nx, ny, 128, 2 * chans), bf16)],
        compiler_params=params,
        name="coarse",
    )(
        full, w_in9, w_mid9, w_lift, mid_back, in_back
    )

    near = pltpu.VMEM((6, 6, 3 * chans, 128), bf16)
    block = (2 * chans // (ny * nz), 27 * ci)
    output, grad_input, parts = pl.pallas_call(
        lambda *refs: last_kernel(counts, *refs),
        out_shape=(
            shape((4, 4, chans, 128), bf16),
            shape((4, 4, chans, 128), bf16),
            shape((total,) + block, bf16),
        ),
        in_specs=vmem(6),
        out_specs=vmem(3),
        scratch_shapes=[
            near,
            near,
            near,
            pltpu.VMEM((2, 27 * chans, chans), f32),
            pltpu.VMEM((2, chans, 27 * chans), bf16),
        ],
        compiler_params=params,
        name="last",
    )(ext, z_first, d_joined, grown, w_fine_out, w_fine_in)

    (sums,) = spread_call(
        lambda *refs: sum_kernel(counts, scale, *refs),
        counts,
        1,
        (shape(block, f32),),
        [pltpu.VMEM((total,) + block, bf16)],
        "sum_parts",
        parts,
    )
    sums = sums.reshape(2, -1, 27, ci).transpose(0, 2, 3, 1)

    def owned(grad):
        return grad.reshape(9, grad.shape[1], 3, -1).transpose(0, 2, 3, 1).reshape(
            27, -1, grad.shape[1]
        )

    return (
        output.transpose(2, 0, 1, 3),
        grad_input.transpose(2, 0, 1, 3),
        sums[1],
        owned(g_in),
        owned(g_mid),
        g_lift.T,
        sums[0],
    )


def choose(features, *rest):
    nx, ny, nz = (lax.axis_size(axis) for axis in AXES)
    total = nx * ny * nz
    wide = rest[4].shape[0]
    fits = features.shape == (32, 4, 4, 128) and nz == 4 and total <= DIRECT
    fits = fits and 32 % (ny * nz) == 0 and 32 % nx == 0 and 32 // nx == 8 and wide == 128
    return (shards if fits else shards_layered)(features, *rest)


def solution(mesh):
    whole = P(None, "gx", "gy", "gz")
    split = P(None, "gx", ("gy", "gz"))
    return jax.shard_map(
        choose,
        mesh=mesh,
        in_specs=(whole, whole, P(), P(), P(), P(), P()),
        out_specs=(whole, whole, split, split, split, P("gx", ("gy", "gz")), split),
        check_vma=False,
    )
```

```python
import math

import jax
import jax.numpy as jnp
from jax import lax
from jax.experimental import pallas as pl
from jax.experimental.pallas import tpu as pltpu
from jax.sharding import PartitionSpec as P

AXES = ("gx", "gy", "gz")
MESH = pl.DeviceIdType.MESH
DIRECT = 64


def place(flat, counts):
    nx, ny, nz = counts
    return (flat // (ny * nz), (flat // nz) % ny, flat % nz)


def meet(counts, total, me):
    barrier = pltpu.get_barrier_semaphore()

    def greet(k, carry):
        pl.semaphore_signal(
            barrier, inc=1, device_id=place((me + k) % total, counts), device_id_type=MESH
        )
        return carry

    lax.fori_loop(1, total, greet, 0)
    pl.semaphore_wait(barrier, total - 1)


def spread_kernel(counts, each, x_ref, o_ref, local_sem, send_sem, recv_sem, during):
    total = counts[0] * counts[1] * counts[2]
    me = (lax.axis_index("gx") * counts[1] + lax.axis_index("gy")) * counts[2] + lax.axis_index(
        "gz"
    )
    meet(counts, total, me)

    def copy(k):
        peer = (me + k) % total
        return pltpu.make_async_remote_copy(
            src_ref=x_ref.at[peer] if each else x_ref,
            dst_ref=o_ref.at[me],
            send_sem=send_sem.at[k],
            recv_sem=recv_sem.at[k],
            device_id=place(peer, counts),
            device_id_type=MESH,
        )

    def begin(k, carry):
        copy(k).start()
        return carry

    def finish(k, carry):
        copy(k).wait()
        return carry

    lax.fori_loop(1, total, begin, 0)
    own = pltpu.make_async_copy(x_ref.at[me] if each else x_ref, o_ref.at[me], local_sem)
    own.start()
    during()
    own.wait()
    lax.fori_loop(1, total, finish, 0)


def gather_kernel(counts, x_ref, w_mid, w_in, o_ref, mid_back, in_back, *sems):
    wide, narrow = w_mid.shape[2], in_back.shape[2]

    def turn():
        def body(ab, carry):
            for c in range(3):
                rows = slice(c * wide, c * wide + wide)
                mid_back[ab, rows, :] = w_mid[8 - ab, (2 - c) * wide : (3 - c) * wide, :].T
                in_back[ab, rows, :] = w_in[8 - ab, (2 - c) * narrow : (3 - c) * narrow, :].T
            return carry

        lax.fori_loop(0, 9, body, 0)

    spread_kernel(counts, False, x_ref, o_ref, *sems, turn)


def sum_kernel(counts, scale, x_ref, o_ref, landed, *sems):
    spread_kernel(counts, True, x_ref, landed, *sems, lambda: None)
    o_ref[...] = landed[...].astype(jnp.float32).sum(0) * scale


def spread_call(kernel, counts, ident, outs, scratch, name, *args):
    total = counts[0] * counts[1] * counts[2]
    return pl.pallas_call(
        kernel,
        out_shape=outs,
        in_specs=vmem(len(args)),
        out_specs=vmem(len(outs)),
        scratch_shapes=scratch
        + [
            pltpu.SemaphoreType.DMA,
            pltpu.SemaphoreType.DMA((total,)),
            pltpu.SemaphoreType.DMA((total,)),
        ],
        compiler_params=pltpu.CompilerParams(collective_id=ident, has_side_effects=True),
        name=name,
    )(*args)


def extended(cells, sides, width):
    for axis, dim in sides:
        count = lax.axis_size(axis)
        ends = count - 1
        head = lax.slice_in_dim(cells, 0, width, axis=dim)
        tail = lax.slice_in_dim(cells, cells.shape[dim] - width, cells.shape[dim], axis=dim)
        cells = jnp.concatenate(
            [
                lax.ppermute(tail, axis, [(i, (i + 1) % count) for i in range(ends)]),
                cells,
                lax.ppermute(head, axis, [((i + 1) % count, i) for i in range(ends)]),
            ],
            axis=dim,
        )
    return cells


def silu_slope(values):
    sigma = jax.nn.sigmoid(values)
    return sigma * (1.0 + values * (1.0 - sigma))


def conv_valid(padded, weight, form="NCDHW"):
    kernel = weight.reshape(3, 3, 3, weight.shape[1], weight.shape[2])
    result = lax.conv_general_dilated(
        padded[None],
        kernel,
        (1, 1, 1),
        "VALID",
        dimension_numbers=(form, "DHWIO", form),
        preferred_element_type=jnp.float32,
    )
    return result[0]


def flipped(weight):
    return jnp.flip(weight, 0).transpose(0, 2, 1)


def pool_blocks(field):
    chans, depth, height, length = field.shape
    grouped = field.astype(jnp.float32).reshape(
        chans, depth // 4, 4, height // 4, 4, length // 4, 4
    )
    return grouped.sum(axis=(2, 4, 6))


def spread_up(field):
    chans, depth, height, length = field.shape
    grown = jnp.broadcast_to(
        field[:, :, None, :, None, :, None], (chans, depth, 4, height, 4, length, 4)
    )
    return grown.reshape(chans, depth * 4, height * 4, length * 4)


def tap_grad_direct(padded, grad):
    depth = padded.shape[1] - 2
    height = padded.shape[2] - 2
    length = padded.shape[3] - 2
    flat_grad = grad.reshape(grad.shape[0], -1)
    blocks = []
    for tap in range(27):
        shift_x, shift_y, shift_z = (tap // 9, tap // 3 % 3, tap % 3)
        window = padded[
            :, shift_x : shift_x + depth, shift_y : shift_y + height, shift_z : shift_z + length
        ].reshape(padded.shape[0], -1)
        blocks.append(
            lax.dot_general(
                window, flat_grad, (((1,), (1,)), ((), ())), preferred_element_type=jnp.float32
            )
        )
    return jnp.stack(blocks)


def fine_rim(field):
    return extended(field, (("gx", 1), ("gy", 2), ("gz", 3)), 1)


def coarse_rim(field):
    return extended(field, (("gx", 1), ("gy", 2), ("gz", 3)), 1)


def reduce_grad(partial_value):
    first = lax.psum_scatter(partial_value, "gx", scatter_dimension=1, tiled=True)
    return lax.psum_scatter(first, ("gy", "gz"), scatter_dimension=2, tiled=True)


def input_share(field):
    parts = lax.all_to_all(field[None], "gx", split_axis=1, concat_axis=0, tiled=True)
    moved = jnp.moveaxis(parts, 0, 1)
    moved = moved.reshape(moved.shape[0], -1, moved.shape[3], moved.shape[4])
    moved = lax.all_gather(moved, "gy", axis=2, tiled=True)
    return lax.all_gather(moved, "gz", axis=3, tiled=True)


def output_share(field):
    parts = lax.all_to_all(field[None], ("gy", "gz"), split_axis=1, concat_axis=0, tiled=True)
    count_y = lax.axis_size("gy")
    count_z = lax.axis_size("gz")
    chans = parts.shape[1]
    depth, height, length = (parts.shape[2], parts.shape[3], parts.shape[4])
    grid = parts.reshape(count_y, count_z, chans, depth, height, length).transpose(2, 3, 0, 4, 1, 5)
    grid = grid.reshape(chans, depth, count_y * height, count_z * length)
    return lax.all_gather(grid, "gx", axis=1, tiled=True)


def shards_layered(features, cotangent, w_fine_in, w_coarse_in, w_coarse_mid, w_lift, w_fine_out):
    depth, height, length = (features.shape[1], features.shape[2], features.shape[3])
    whole_cells = (
        depth * lax.axis_size("gx") * height * lax.axis_size("gy") * length * lax.axis_size("gz")
    )
    scale = 1.0 / math.sqrt(whole_cells)
    padded_in = fine_rim(features)
    z_first = conv_valid(padded_in, w_fine_in)
    act_first = jax.nn.silu(z_first).astype(jnp.bfloat16)
    pooled = (pool_blocks(act_first) / 64.0).astype(jnp.bfloat16)
    pooled_pad = coarse_rim(pooled)
    z_second = conv_valid(pooled_pad, w_coarse_in)
    act_second = jax.nn.silu(z_second).astype(jnp.bfloat16)
    second_pad = coarse_rim(act_second)
    z_third = conv_valid(second_pad, w_coarse_mid)
    act_third = jax.nn.silu(z_third).astype(jnp.bfloat16)
    lifted = lax.dot_general(
        w_lift, act_third, (((0,), (0,)), ((), ())), preferred_element_type=jnp.float32
    )
    joined = (act_first.astype(jnp.float32) + spread_up(lifted)).astype(jnp.bfloat16)
    padded_joined = fine_rim(joined)
    output = conv_valid(padded_joined, w_fine_out).astype(jnp.bfloat16)
    part_fine_out = tap_grad_direct(padded_joined, cotangent) * scale
    d_joined = conv_valid(fine_rim(cotangent), flipped(w_fine_out))
    d_lift = pool_blocks(d_joined)
    lift_partial = (
        lax.dot_general(
            act_third.astype(jnp.float32),
            d_lift,
            (((1, 2, 3), (1, 2, 3)), ((), ())),
            precision=lax.Precision.HIGHEST,
        )
        * scale
    )
    d_third = lax.dot_general(
        w_lift.astype(jnp.float32),
        d_lift,
        (((1,), (0,)), ((), ())),
        precision=lax.Precision.HIGHEST,
    )
    dz_third = (d_third * silu_slope(z_third)).astype(jnp.bfloat16)
    dz_third_pad = coarse_rim(dz_third)
    grad_coarse_mid = None
    sources = input_share(act_second)
    sources_pad = jnp.pad(sources, ((0, 0), (1, 1), (1, 1), (1, 1)))
    targets = output_share(dz_third)
    grad_coarse_mid = tap_grad_direct(sources_pad, targets) * scale
    dz_second = (conv_valid(dz_third_pad, flipped(w_coarse_mid)) * silu_slope(z_second)).astype(
        jnp.bfloat16
    )
    dz_second_pad = coarse_rim(dz_second)
    part_coarse_in = tap_grad_direct(pooled_pad, dz_second) * scale
    d_pool = conv_valid(dz_second_pad, flipped(w_coarse_in))
    dz_first = ((d_joined + spread_up(d_pool) / 64.0) * silu_slope(z_first)).astype(jnp.bfloat16)
    part_fine_in = tap_grad_direct(padded_in, dz_first) * scale
    grad_input = conv_valid(fine_rim(dz_first), flipped(w_fine_in)).astype(jnp.bfloat16)
    pending = [part_fine_out, lift_partial[None], part_coarse_in, part_fine_in]
    reduced = [reduce_grad(partial_value) for partial_value in pending]
    grad_fine_out = reduced[0]
    grad_lift = reduced[1][0]
    grad_coarse_in = reduced[2]
    grad_fine_in = reduced[3]
    return (
        output,
        grad_input,
        grad_fine_in,
        grad_coarse_in,
        grad_coarse_mid,
        grad_lift,
        grad_fine_out,
    )


def halo_kernel(counts, x_ref, o_ref, rows, packed, from_low, from_high, sends, recvs):
    nx, ny, nz = counts
    gx, gy, gz = (lax.axis_index(axis) for axis in AXES)
    sides = [(i, j, 0) for i in (-1, 0, 1) for j in (-1, 0, 1) if (i, j) != (0, 0)]
    sides += [(0, 0, -1), (0, 0, 1)]

    def there(side, sign):
        x, y, z = gx + sign * side[0], gy + sign * side[1], gz + sign * side[2]
        real = (x >= 0) & (x < nx) & (y >= 0) & (y < ny) & (z >= 0) & (z < nz)
        return (x, y, z), real

    rows[...] = jnp.zeros_like(rows)
    from_low[...] = jnp.zeros_like(from_low)
    from_high[...] = jnp.zeros_like(from_high)
    barrier = pltpu.get_barrier_semaphore()
    met = 0
    for side in sides:
        peer, real = there(side, 1)
        met = met + jnp.where(real, 1, 0)

        @pl.when(real)
        def _():
            pl.semaphore_signal(barrier, inc=1, device_id=peer, device_id_type=MESH)

    pl.semaphore_wait(barrier, met)
    d, h = x_ref.shape[:2]
    take = {-1: lambda n: pl.ds(0, 2), 0: lambda n: pl.ds(0, n), 1: lambda n: pl.ds(n - 2, 2)}
    land = {-1: lambda n: pl.ds(n + 2, 2), 0: lambda n: pl.ds(2, n), 1: lambda n: pl.ds(0, 2)}

    def transfer(k, side):
        if k < 8:
            source = x_ref.at[take[side[0]](d), take[side[1]](h)]
            target = rows.at[land[side[0]](d), land[side[1]](h)]
        else:
            source, target = packed, (from_high if side[2] < 0 else from_low)
        return pltpu.make_async_remote_copy(
            src_ref=source,
            dst_ref=target,
            send_sem=sends.at[k],
            recv_sem=recvs.at[k],
            device_id=there(side, 1)[0],
            device_id_type=MESH,
        )

    def run(first, last):
        for k in range(first, last):

            @pl.when(there(sides[k], 1)[1])
            def _():
                transfer(k, sides[k]).start()

    def settle(first, last):
        for k in range(first, last):

            @pl.when(there(sides[k], -1)[1])
            def _():
                transfer(k, sides[k]).wait_recv()

            @pl.when(there(sides[k], 1)[1])
            def _():
                transfer(k, sides[k]).wait_send()

    run(0, 8)
    settle(0, 8)
    rows[2 : 2 + d, 2 : 2 + h] = x_ref[...]
    lane = lax.broadcasted_iota(jnp.int32, (x_ref.shape[2], 128), 1)
    spots = [(x, y) for x in range(d + 4) for y in range(h + 4)]
    for part in range(2):
        group = jnp.zeros(lane.shape, jnp.float32)
        for r in range(32):
            x, y = spots[part * 32 + r]
            turned = pltpu.roll(rows[x, y].astype(jnp.float32), (2 + 4 * r) % 128, 1)
            group = jnp.where(lane // 4 == r, turned, group)
        packed[:, part * 128 : part * 128 + 128] = group.astype(jnp.bfloat16)
    run(8, 10)
    for x, y in spots:
        o_ref[x, y, :, 0:128] = rows[x, y]
    settle(8, 10)
    for part in range(2):
        span = slice(part * 128, part * 128 + 128)
        group = jnp.where(
            lane % 4 >= 2,
            from_high[:, span].astype(jnp.float32),
            from_low[:, span].astype(jnp.float32),
        )
        for r in range(32):
            x, y = spots[part * 32 + r]
            o_ref[x, y, :, 128:256] = pltpu.roll(group, 126 - 4 * r if r < 32 else 0, 1).astype(
                jnp.bfloat16
            )


def vmem(count):
    return [pl.BlockSpec(memory_space=pltpu.VMEM)] * count


ROOMY = 60 * 1024 * 1024


def halo(x, counts, ident):
    d, h, chans, length = x.shape
    edge = pltpu.VMEM((chans, 256), jnp.bfloat16)
    return pl.pallas_call(
        lambda *refs: halo_kernel(counts, *refs),
        out_shape=jax.ShapeDtypeStruct((d + 4, h + 4, chans, 256), x.dtype),
        in_specs=vmem(1),
        out_specs=vmem(1)[0],
        scratch_shapes=[
            pltpu.VMEM((d + 4, h + 4, chans, length), x.dtype),
            edge,
            edge,
            edge,
            pltpu.SemaphoreType.DMA((10,)),
            pltpu.SemaphoreType.DMA((10,)),
        ],
        compiler_params=pltpu.CompilerParams(
            collective_id=ident, has_side_effects=True, vmem_limit_bytes=ROOMY
        ),
        name="halo",
    )(x)


def stacked(value):
    size = value.shape[1]
    return jnp.concatenate(
        [pltpu.roll(value, 1, 1), value, pltpu.roll(value, size - 1, 1)]
    ).astype(jnp.bfloat16)


def around(ref, x, y, rows, lanes):
    return jnp.concatenate(
        [ref[x + a, y + b, rows, lanes] for a in range(3) for b in range(3)]
    )


def dot(a, b):
    return jnp.dot(a, b, preferred_element_type=jnp.float32)


def dot_over(a, b, dims, precision=None):
    return lax.dot_general(
        a, b, ((dims[:1], dims[1:]), ((), ())), precision=precision, preferred_element_type=jnp.float32
    )


def ahead(weight):
    return weight[...].reshape(27 * weight.shape[1], weight.shape[2]).T


def back(weight):
    return jnp.concatenate([weight[26 - t] for t in range(27)], axis=1)


def grouped(count, size, body):
    def several(g, carry):
        for i in range(size):
            body(g * size + i, carry)
        return carry

    lax.fori_loop(0, count // size, several, 0)


def fine_kernel(ext, w_in, w_out, z_ref, d_ref, mine, taps, total, ws):
    ws[0], ws[1] = ahead(w_in), back(w_out)

    def fill(r, carry):
        x, y = r // 8, r % 8
        for f in range(2):
            value = ext[x, y, f * 32 : f * 32 + 32, :].astype(jnp.float32)
            taps[x, y, f * 96 : f * 96 + 96, :] = stacked(value)
        return carry

    grouped(64, 4, fill)
    total[...] = jnp.zeros_like(total)

    def body(r, carry):
        x, y = r // 6, r % 6
        z = dot(ws[0], around(taps, x, y, slice(0, 96), slice(None)))
        d = dot(ws[1], around(taps, x, y, slice(96, 192), slice(None)))
        z_ref[x, y] = z
        d_ref[x, y] = d
        act = jax.nn.silu(z[:, :128]).astype(jnp.bfloat16).astype(jnp.float32)
        own = jnp.where((x >= 1) & (x <= 4) & (y >= 1) & (y <= 4), 1.0, 0.0)
        total[...] += own * jnp.concatenate([act, d[:, :128]])
        return carry

    grouped(36, 6, body)
    row = lax.broadcasted_iota(jnp.int32, (32, 128), 0)
    lane = lax.broadcasted_iota(jnp.int32, (32, 128), 1)
    pick = jnp.where(lane // 4 == row, 1.0, 0.0)
    sums = dot_over(pick, total[...], (1, 1), lax.Precision.HIGHEST)
    both = jnp.concatenate([sums[:, :32] * (1.0 / 64.0), sums[:, 32:]], axis=1)
    mine[...] = jnp.concatenate([both[:16], both[16:]], axis=1).astype(jnp.bfloat16)


def coarse_kernel(
    counts, scale, full, w_in, w_mid, w_lift, w_mid_back, w_in_back,
    grown, g_mid, g_in, g_lift,
    pad_in, pad_mid, pad_smid, pad_sin, table,
):
    nx, ny, nz = counts
    cells = nx * ny * 128
    gx, gy, gz = (lax.axis_index(axis) for axis in AXES)
    for pad in (pad_in, pad_mid, pad_smid, pad_sin):
        pad[...] = jnp.zeros_like(pad)

    def pick(size, parts, index):
        each = size // parts
        row = lax.broadcasted_iota(jnp.int32, (size, each), 0)
        column = lax.broadcasted_iota(jnp.int32, (size, each), 1)
        return jnp.where(row == index * each + column, 1.0, 0.0).astype(jnp.bfloat16)

    at_o = gy * nz + gz
    pick_mid, pick_in = pick(128, nx, gx), pick(32, nx, gx)
    pick_o, pick_lift = pick(128, ny * nz, at_o), pick(32, ny * nz, at_o)

    def fill(pad, value):
        at = lax.broadcasted_iota(jnp.int32, value.shape, 0) % 128
        low = jnp.where(at == 0, 0.0, pltpu.roll(value, 1, 0))
        high = jnp.where(at == 127, 0.0, pltpu.roll(value, cells - 1, 0))
        wide = jnp.concatenate([low, value, high], axis=1).astype(jnp.bfloat16)
        pad[1 : nx + 1, 1 : ny + 1] = wide.reshape(nx, ny, 128, wide.shape[1])

    def window(pad, ab):
        a, b = ab // 3, ab % 3
        return pad[a : a + nx, b : b + ny].reshape(cells, pad.shape[3])

    def conv(pad, weight):
        result = dot(window(pad, 0), weight[0])
        for ab in range(1, 9):
            result = result + dot(window(pad, ab), weight[ab])
        return result

    def slope(v):
        sigma = jax.nn.sigmoid(v)
        return sigma * (1.0 + v * (1.0 - sigma))

    pieces = []
    for k in range(nx * ny):
        for z in range(nz):
            block = full[k * nz + z]
            pieces += [block[:, :64], block[:, 64:]]
    both = jnp.concatenate(pieces)
    pooled, d_lift = both[:, :32], both[:, 32:]
    fill(pad_in, pooled.astype(jnp.float32))
    z_second = conv(pad_in, w_in)
    act_second = jax.nn.silu(z_second)
    fill(pad_mid, act_second)
    z_third = conv(pad_mid, w_mid)
    act_third = jax.nn.silu(z_third).astype(jnp.bfloat16)
    lifted = dot(act_third, w_lift[...])
    dz_third = (dot_over(d_lift, w_lift[...], (1, 1)) * slope(z_third)).astype(jnp.bfloat16)
    fill(pad_mid, dz_third.astype(jnp.float32))
    dz_second = (conv(pad_mid, w_mid_back) * slope(z_second)).astype(jnp.bfloat16)
    fill(pad_mid, dz_second.astype(jnp.float32))
    d_pool = conv(pad_mid, w_in_back)

    table[...] = (
        jnp.concatenate([lifted, d_pool * (1.0 / 64.0)], axis=1)
        .astype(jnp.bfloat16)
        .reshape(nx, ny, 128, 64)
    )
    row = lax.broadcasted_iota(jnp.int32, (128, 256), 0)
    lane = lax.broadcasted_iota(jnp.int32, (128, 256), 1)
    cell = jnp.where(lane < 192, lane // 4, -1) + gz * 32
    grow = jnp.where(row == cell, 1.0, 0.0).astype(jnp.bfloat16)
    for i in range(3):
        for j in range(3):
            x = jnp.clip(gx + i - 1, 0, nx - 1)
            y = jnp.clip(gy + j - 1, 0, ny - 1)
            grown[i, j] = dot_over(table[x, y], grow, (0, 0))

    third_o = dot(dz_third, pick_o).T.astype(jnp.bfloat16)
    second_o = dot(dz_second, pick_o).T.astype(jnp.bfloat16)
    fill(pad_smid, dot(act_second.astype(jnp.bfloat16), pick_mid))
    fill(pad_sin, dot(pooled, pick_in))
    for ab in range(9):
        g_mid[ab] = dot(third_o, window(pad_smid, ab)) * scale
        g_in[ab] = dot(second_o, window(pad_sin, ab)) * scale
    third_i = dot(act_third, pick_mid).astype(jnp.bfloat16)
    lift_o = dot(d_lift, pick_lift).T.astype(jnp.bfloat16)
    g_lift[...] = dot(lift_o, third_i) * scale


def last_kernel(
    counts, ext, z_ref, d_ref, grown, w_out, w_in, out, g_input, parts, tj, td, tf, sums, ws
):
    ws[0], ws[1] = ahead(w_out), back(w_in)
    nx, ny, nz = counts
    gx, gy, gz = (lax.axis_index(axis) for axis in AXES)
    lane = lax.broadcasted_iota(jnp.int32, (32, 256), 1)
    at_z = gz * 128 + jnp.where(lane < 192, lane, lane - 256)
    keep_z = jnp.where((at_z >= 0) & (at_z < nz * 128), 1.0, 0.0)

    def fill(r, carry):
        x, y = r // 6, r % 6
        at_x, at_y = gx * 4 + x - 1, gy * 4 + y - 1
        real = (at_x >= 0) & (at_x < nx * 4) & (at_y >= 0) & (at_y < ny * 4)
        keep = keep_z * jnp.where(real, 1.0, 0.0)
        up = grown[(x + 3) // 4, (y + 3) // 4]
        z = z_ref[x, y]
        sigma = jax.nn.sigmoid(z)
        act = (z * sigma).astype(jnp.bfloat16).astype(jnp.float32)
        joined = (act + up[:32]).astype(jnp.bfloat16).astype(jnp.float32) * keep
        dz = (d_ref[x, y] + up[32:]) * (sigma * (1.0 + z * (1.0 - sigma))) * keep
        dz = dz.astype(jnp.bfloat16).astype(jnp.float32)
        tj[x, y] = stacked(joined)[:, :128]
        td[x, y] = stacked(dz)[:, :128]
        tf[x, y] = stacked(ext[x + 1, y + 1, 0:32, :].astype(jnp.float32))[:, :128]
        return carry

    grouped(36, 3, fill)
    sums[...] = jnp.zeros_like(sums)

    def body(r, carry):
        x, y = r // 2, (r % 2) * 2
        whole = slice(None)

        def pair(ref):
            return jnp.concatenate(
                [around(ref, x, y, whole, whole), around(ref, x, y + 1, whole, whole)], axis=1
            )

        near = pair(tj)
        result = dot(ws[0], near).astype(jnp.bfloat16)
        out[x, y], out[x, y + 1] = result[:, :128], result[:, 128:]
        cot = jnp.concatenate(
            [ext[x + 2, y + 2, 32:64, 0:128], ext[x + 2, y + 3, 32:64, 0:128]], axis=1
        )
        sums[0] += dot_over(near, cot, (1, 1))
        result = dot(ws[1], pair(td)).astype(jnp.bfloat16)
        g_input[x, y], g_input[x, y + 1] = result[:, :128], result[:, 128:]
        grad = jnp.concatenate(
            [td[x + 1, y + 1, 32:64, :], td[x + 1, y + 2, 32:64, :]], axis=1
        )
        sums[1] += dot_over(pair(tf), grad, (1, 1))
        return carry

    grouped(8, 2, body)
    ci, co = 32 // nx, 32 // (ny * nz)
    for f in range(2):
        value = sums[f].reshape(27, nx, ci, 32)
        for i in range(nx):
            block = value[:, i].reshape(27 * ci, 32).T
            for j in range(ny * nz):
                parts[i * ny * nz + j, f * co : f * co + co, 0 : 27 * ci] = block[
                    j * co : j * co + co
                ].astype(jnp.bfloat16)


def shards(features, cotangent, w_fine_in, w_coarse_in, w_coarse_mid, w_lift, w_fine_out):
    counts = tuple(lax.axis_size(axis) for axis in AXES)
    nx, ny, nz = counts
    total = nx * ny * nz
    chans, depth, height, length = features.shape
    wide = w_lift.shape[0]
    scale = 1.0 / math.sqrt(total * depth * height * length)
    f32, bf16 = jnp.float32, jnp.bfloat16
    shape = jax.ShapeDtypeStruct
    params = pltpu.CompilerParams(vmem_limit_bytes=ROOMY)

    rows = jnp.concatenate([features, cotangent]).transpose(1, 2, 0, 3)
    ext = halo(rows, counts, 2)
    field = shape((6, 6, chans, 256), f32)
    z_first, d_joined, mine = pl.pallas_call(
        fine_kernel,
        out_shape=(field, field, shape((16, 128), bf16)),
        in_specs=vmem(3),
        out_specs=vmem(3),
        scratch_shapes=[
            pltpu.VMEM((8, 8, 192, 256), bf16),
            pltpu.VMEM((64, 128), f32),
            pltpu.VMEM((2, chans, 27 * chans), bf16),
        ],
        compiler_params=params,
        name="fine",
    )(ext, w_fine_in, w_fine_out)

    w_in9 = w_coarse_in.reshape(9, 3 * chans, wide)
    w_mid9 = w_coarse_mid.reshape(9, 3 * wide, wide)
    full, mid_back, in_back = spread_call(
        lambda *refs: gather_kernel(counts, *refs),
        counts,
        0,
        (
            shape((total,) + mine.shape, bf16),
            shape(w_mid9.shape, bf16),
            shape((9, 3 * wide, chans), bf16),
        ),
        [],
        "gather",
        mine,
        w_mid9,
        w_in9,
    )

    co, cw = wide // (ny * nz), wide // nx
    ci = chans // nx
    pads = [3 * chans, 3 * wide, 3 * cw, 3 * ci]
    grown, g_mid, g_in, g_lift = pl.pallas_call(
        lambda *refs: coarse_kernel(counts, scale, *refs),
        out_shape=(
            shape((3, 3, 2 * chans, 256), f32),
            shape((9, co, 3 * cw), f32),
            shape((9, co, 3 * ci), f32),
            shape((chans // (ny * nz), cw), f32),
        ),
        in_specs=vmem(6),
        out_specs=vmem(4),
        scratch_shapes=[pltpu.VMEM((nx + 2, ny + 2, 128, k), bf16) for k in pads]
        + [pltpu.VMEM((nx, ny, 128, 2 * chans), bf16)],
        compiler_params=params,
        name="coarse",
    )(
        full, w_in9, w_mid9, w_lift, mid_back, in_back
    )

    near = pltpu.VMEM((6, 6, 3 * chans, 128), bf16)
    block = (2 * chans // (ny * nz), 27 * ci)
    output, grad_input, parts = pl.pallas_call(
        lambda *refs: last_kernel(counts, *refs),
        out_shape=(
            shape((4, 4, chans, 128), bf16),
            shape((4, 4, chans, 128), bf16),
            shape((total,) + block, bf16),
        ),
        in_specs=vmem(6),
        out_specs=vmem(3),
        scratch_shapes=[
            near,
            near,
            near,
            pltpu.VMEM((2, 27 * chans, chans), f32),
            pltpu.VMEM((2, chans, 27 * chans), bf16),
        ],
        compiler_params=params,
        name="last",
    )(ext, z_first, d_joined, grown, w_fine_out, w_fine_in)

    (sums,) = spread_call(
        lambda *refs: sum_kernel(counts, scale, *refs),
        counts,
        1,
        (shape(block, f32),),
        [pltpu.VMEM((total,) + block, bf16)],
        "sum_parts",
        parts,
    )
    sums = sums.reshape(2, -1, 27, ci).transpose(0, 2, 3, 1)

    def owned(grad):
        return grad.reshape(9, grad.shape[1], 3, -1).transpose(0, 2, 3, 1).reshape(
            27, -1, grad.shape[1]
        )

    return (
        output.transpose(2, 0, 1, 3),
        grad_input.transpose(2, 0, 1, 3),
        sums[1],
        owned(g_in),
        owned(g_mid),
        g_lift.T,
        sums[0],
    )


def choose(features, *rest):
    nx, ny, nz = (lax.axis_size(axis) for axis in AXES)
    total = nx * ny * nz
    wide = rest[4].shape[0]
    fits = features.shape == (32, 4, 4, 128) and nz == 4 and total <= DIRECT
    fits = fits and 32 % (ny * nz) == 0 and 32 % nx == 0 and 32 // nx == 8 and wide == 128
    return (shards if fits else shards_layered)(features, *rest)


def solution(mesh):
    whole = P(None, "gx", "gy", "gz")
    split = P(None, "gx", ("gy", "gz"))
    return jax.shard_map(
        choose,
        mesh=mesh,
        in_specs=(whole, whole, P(), P(), P(), P(), P()),
        out_specs=(whole, whole, split, split, split, P("gx", ("gy", "gz")), split),
        check_vma=False,
    )
```
